256 devices in a mesh: seg: 4 (over y), ep: 64 (over z, x, core).
Axes of the slice: x: 4, y: 4, z: 8, core: 2. Of those that a mesh axis runs over, the one named last changes fastest.
Arguments:
- frames_in: bfloat16 [32768, 2048], P(('seg', 'ep')), may hold values from -36 to 36
- expert_ids: int32 [32768, 6], P(('seg', 'ep')), may hold values from 0 to 63, all different within a row
- gate_values: float32 [32768, 6], P(('seg', 'ep')), may hold values from 0.02 to 0.3
- gate_weight: bfloat16 [64, 2048, 768], P('ep'), may hold values from -0.125 to 0.125
- up_weight: bfloat16 [64, 2048, 768], P('ep'), may hold values from -0.125 to 0.125
- down_weight: bfloat16 [64, 768, 2048], P('ep'), may hold values from -0.21875 to 0.21875
- norm_gain: float32 [2048], replicated, may hold values from 0.5 to 1.5
- pose_weight: bfloat16 [2048, 256], replicated, may hold values from -0.125 to 0.125
- target_pose: float32 [32768, 256], P(('seg', 'ep')), may hold values from -6 to 6
- foot_contact: int32 [32768, 4], P(('seg', 'ep')), may hold values 0 or 1
Outputs:
- grad_input: bfloat16 [32768, 2048], P(('seg', 'ep'))
- grad_gates: float32 [32768, 6], P(('seg', 'ep'))
- loss_value: float32 [], replicated
The draws below stay inside these ranges and needn't reach their ends.
Inputs may be any that keep to these rules, and one draw needn't show every extreme that they name: `expert_ids`: each row names 6 different experts.
All inputs are finite; a program needn't handle non-finite values. No bound on the sum of `foot_contact` on one device may be relied on, other than what follows from the above.
Results may differ from the reference program's by a relative error of at most 0.011.
Values may be sent and summed in bfloat16 or wider, within the bound.
A program may use at most 128 MiB of HBM per device.

```python
import math
import jax
import jax.numpy as jnp
from jax import lax

D = 2048
FFW = 768
POSE = 256
FEET = 4
TOP = 6
TOK_DEV = 128
EXPERTS = 64
CAP = 12
FRAMES = 32768


def draw_frames_in(key, part):
    base_key, row_key, column_key = jax.random.split(key, 3)
    row_scale = jnp.exp(jax.random.uniform(row_key, (FRAMES, 1), jnp.float32, math.log(0.3), math.log(3.0)))
    column_scale = jnp.exp(jax.random.uniform(column_key, (1, D), jnp.float32, math.log(0.3), math.log(3.0)))
    base_rows = jnp.clip(jax.random.normal(base_key, (FRAMES, D), jnp.float32), -4.0, 4.0)
    return (base_rows * row_scale * column_scale).astype(jnp.bfloat16)


def set_ends(drawn, own_key, least, top_value):
    place = [jax.random.randint(jax.random.fold_in(own_key, axis), (), 0, length) for axis, length in enumerate(drawn.shape)]
    longest = drawn.shape.index(max(drawn.shape))
    neighbour = place[:longest] + [(place[longest] + 1) % drawn.shape[longest]] + place[longest + 1:]
    return drawn.at[tuple(place)].set(least).at[tuple(neighbour)].set(top_value)


def block_levels(key, shape, shards, least, high):
    gain = 1.0
    for dim, blocks in shards:
        heights = jax.random.uniform(jax.random.fold_in(jax.random.fold_in(key, 6), dim), (blocks,), jnp.float32, least / len(shards), high / len(shards))
        gain = gain * jnp.repeat(jnp.exp(heights), shape[dim] // blocks).reshape((-1,) + (1,) * (len(shape) - 1 - dim))
    return gain


def picks_of(own_key, rows, number_of, top, lift):
    order = jax.random.permutation(jax.random.fold_in(own_key, 1), number_of)
    boost = order
    for power in range(3):
        boost = boost * boost // number_of
    boost = boost * lift // number_of
    lots = jax.random.randint(jax.random.fold_in(own_key, 2), (rows, number_of), 0, 4096) + boost
    sure = jax.random.permutation(jax.random.fold_in(own_key, 3), rows)[jnp.arange(number_of) % rows]
    lots = jnp.where(jnp.arange(rows)[:, None] == sure[None, :], 1 << 14, lots)
    score = lots * number_of + jnp.arange(number_of)
    return lax.top_k(score.astype(jnp.int32), top)[1].astype(jnp.int32)


def bell_draw(stream_key, extent, width, reach, pieces=(), kind=jnp.bfloat16):
    gain = block_levels(stream_key, extent, pieces, -0.22, 0.18) if pieces else 1.0
    values = jax.random.normal(stream_key, extent, jnp.float32) * width * gain
    return jnp.minimum(jnp.maximum(values, -reach), reach).astype(kind)


def setup_inputs(seed: int = 0) -> dict:
    seeds = jax.random.split(jax.random.key(seed), 11)
    return {
        "frames_in": draw_frames_in(jax.random.fold_in(seeds[10], 71), 0),
        "expert_ids": picks_of(seeds[1], FRAMES, EXPERTS, TOP, 1536),
        "gate_values": jnp.clip(jnp.exp(math.log(0.3) - 2.7080503 * jax.random.uniform(seeds[2], (FRAMES, TOP), jnp.float32) ** block_levels(seeds[2], (FRAMES, TOP), ((0, 256),), -0.2, 0.2)), 0.02, 0.3),
        "gate_weight": bell_draw(seeds[3], (EXPERTS, D, FFW), D ** -0.5, 0.125, ((0, 64),)),
        "up_weight": bell_draw(seeds[4], (EXPERTS, D, FFW), D ** -0.5, 0.125, ((0, 64),)),
        "down_weight": bell_draw(seeds[5], (EXPERTS, FFW, D), FFW ** -0.5, 0.21875, ((0, 64),)),
        "norm_gain": jnp.clip(1.0 + 0.1 * jax.random.normal(seeds[6], (D,), jnp.float32), 0.5, 1.5),
        "pose_weight": bell_draw(seeds[7], (D, POSE), D ** -0.5, 0.125),
        "target_pose": bell_draw(seeds[8], (FRAMES, POSE), 1.0, 6.0, ((0, 256),), jnp.float32),
        "foot_contact": set_ends((jax.random.randint(seeds[9], (FRAMES, FEET), 0, 2) < 1).astype(jnp.int32), jax.random.fold_in(seeds[9], 1), 0, 1),
    }


epsilon = 1e-06
foot_weight = 2.0

def silu_parts(pre_act):
    gate_sigmoid = jax.nn.sigmoid(pre_act)
    return (pre_act * gate_sigmoid, gate_sigmoid * (1.0 + pre_act * (1.0 - gate_sigmoid)))

def foot_term(horizon, contact_rep, velocity):
    return foot_weight * horizon[:, None] * contact_rep * velocity

def reference(frames_in, expert_ids, gate_values, gate_weight, up_weight, down_weight, norm_gain, pose_weight, target_pose, foot_contact):
    blocks = FRAMES // TOK_DEV
    block_pairs = TOK_DEV * TOP
    grouped_ids = expert_ids.reshape(blocks, block_pairs)
    onehot = (grouped_ids[:, :, None] == jnp.arange(EXPERTS, dtype=jnp.int32)[None, None, :]).astype(jnp.int32)
    slot_rank = lax.optimization_barrier(jnp.sum((jnp.cumsum(onehot, axis=1) - onehot) * onehot, axis=2))
    kept_mask = slot_rank < CAP
    block_index = jnp.arange(blocks, dtype=jnp.int32)[:, None]
    spare_slot = EXPERTS * blocks * CAP
    position = jnp.where(kept_mask, (grouped_ids * blocks + block_index) * CAP + slot_rank, spare_slot).reshape(-1)
    total_pairs = FRAMES * TOP
    pair_table = jnp.full((spare_slot + 1,), total_pairs, jnp.int32).at[position].set(jnp.arange(total_pairs, dtype=jnp.int32))[:spare_slot]
    pair_table = pair_table.reshape(EXPERTS, blocks * CAP)
    padded_in = jnp.concatenate([frames_in, jnp.zeros((1, D), jnp.bfloat16)], 0)
    flat_gates = jnp.concatenate([gate_values.reshape(-1), jnp.zeros((1,), jnp.float32)], 0)

    def expert_forward(expert):
        pair_rows = pair_table[expert]
        row_block = padded_in[pair_rows // TOP]
        gate_pre = jnp.dot(row_block, gate_weight[expert], preferred_element_type=jnp.float32)
        up_pre = jnp.dot(row_block, up_weight[expert], preferred_element_type=jnp.float32)
        activated, silu_slope = silu_parts(gate_pre)
        hidden = (activated * up_pre).astype(jnp.bfloat16)
        produced = jnp.dot(hidden, down_weight[expert], preferred_element_type=jnp.float32).astype(jnp.bfloat16)
        return (pair_rows, up_pre, activated, silu_slope, produced)

    def add_mixed(mixed_rows, expert):
        pair_rows, up_pre, activated, silu_slope, produced = expert_forward(expert)
        weighted = flat_gates[pair_rows][:, None] * produced.astype(jnp.float32)
        return (mixed_rows.at[pair_rows // TOP].add(weighted, mode='drop'), None)
    mixed_rows, unused = lax.scan(add_mixed, jnp.zeros((FRAMES, D), jnp.float32), jnp.arange(EXPERTS, dtype=jnp.int32))
    state_rows = frames_in.astype(jnp.float32) + mixed_rows
    inverse_rms = lax.rsqrt(lax.optimization_barrier(jnp.mean(state_rows * state_rows, axis=1, keepdims=True)) + epsilon)
    unit_rows = state_rows * inverse_rms
    normed = (unit_rows * norm_gain).astype(jnp.bfloat16)
    pose_out = jnp.dot(normed, pose_weight, preferred_element_type=jnp.float32)
    frame_index = jnp.arange(FRAMES, dtype=jnp.int32)
    horizon = 0.5 + frame_index.astype(jnp.float32) / (FRAMES - 1)
    foot_cols = 3 * FEET
    foot_pos = pose_out[:, :foot_cols]
    contact_rep = jnp.repeat(foot_contact.astype(jnp.float32), 3, axis=1)
    earlier = jnp.concatenate([jnp.zeros((1, foot_cols), jnp.float32), foot_pos[:-1]], 0)
    velocity = jnp.where((frame_index > 0)[:, None], foot_pos - earlier, 0.0)
    foot_pull = foot_term(horizon, contact_rep, velocity)
    pose_error = pose_out - target_pose
    summed = 0.5 * jnp.sum(horizon[:, None] * pose_error * pose_error) + 0.5 * jnp.sum(foot_pull * velocity)
    loss_value = summed / (FRAMES * POSE)
    later_pull = jnp.concatenate([foot_pull[1:], jnp.zeros((1, foot_cols), jnp.float32)], 0)
    grad_pose = horizon[:, None] * pose_error
    grad_pose = jnp.concatenate([grad_pose[:, :foot_cols] + (foot_pull - later_pull), grad_pose[:, foot_cols:]], 1)
    grad_normed = jnp.dot(grad_pose.astype(jnp.bfloat16), pose_weight.T, preferred_element_type=jnp.float32)
    scaled = grad_normed * norm_gain
    grad_state = inverse_rms * (scaled - unit_rows * lax.optimization_barrier(jnp.mean(scaled * unit_rows, axis=1, keepdims=True)))
    moe_grad = grad_state.astype(jnp.bfloat16)
    padded_grad = jnp.concatenate([moe_grad, jnp.zeros((1, D), jnp.bfloat16)], 0)

    def add_grads(totals, expert):
        grad_acc, gate_acc = totals
        pair_rows, up_pre, activated, silu_slope, produced = expert_forward(expert)
        token_rows = pair_rows // TOP
        incoming = padded_grad[token_rows]
        grad_out = (flat_gates[pair_rows][:, None] * incoming).astype(jnp.bfloat16)
        grad_hidden = jnp.dot(grad_out, down_weight[expert].T, preferred_element_type=jnp.float32)
        grad_gate_pre = (grad_hidden * up_pre * silu_slope).astype(jnp.bfloat16)
        grad_up_pre = (grad_hidden * activated).astype(jnp.bfloat16)
        grad_rows = jnp.dot(grad_gate_pre, gate_weight[expert].T, preferred_element_type=jnp.float32)
        grad_rows = (grad_rows + jnp.dot(grad_up_pre, up_weight[expert].T, preferred_element_type=jnp.float32)).astype(jnp.bfloat16)
        grad_acc = grad_acc.at[token_rows].add(grad_rows.astype(jnp.float32), mode='drop')
        slot_dots = lax.optimization_barrier(jnp.sum(incoming.astype(jnp.float32) * produced.astype(jnp.float32), axis=1))
        gate_acc = gate_acc.at[pair_rows].add(slot_dots, mode='drop')
        return ((grad_acc, gate_acc), None)
    totals, unused = lax.scan(add_grads, (grad_state, jnp.zeros((total_pairs,), jnp.float32)), jnp.arange(EXPERTS, dtype=jnp.int32))
    grad_input = totals[0].astype(jnp.bfloat16)
    grad_gates = totals[1].reshape(FRAMES, TOP)
    return (grad_input, grad_gates, loss_value)
```

```python
import functools

import jax
import jax.numpy as jnp
from jax import lax
from jax.experimental import pallas as pl
from jax.experimental.pallas import tpu as pltpu
from jax.sharding import PartitionSpec as P

MESH = pl.DeviceIdType.MESH
epsilon = 1e-06
foot_weight = 2.0

RING = 8
GROUP = 8
ROWS = 128
CAP = 12
TOP = 6
D = 2048
FFW = 768
CHUNK = 512
PAIR = 2 * CAP
BLOCK = GROUP * PAIR
F32 = jnp.float32
BF16 = jnp.bfloat16

PLACE = {0: 0, 1: 1, 7: 2, 2: 3, 6: 4, 3: 5, 5: 6, 4: 7}


def cols(c):
    return pl.ds(c * CHUNK, CHUNK)


class Place:
    def __init__(self):
        ep = lax.axis_index("ep")
        self.z = lax.div(ep, GROUP)
        self.g = lax.rem(ep, GROUP)

    def ring(self, distance):
        return {"ep": lax.rem(self.z + distance + RING, RING) * GROUP + self.g}

    def mate(self, offset):
        return lax.rem(self.g + offset, GROUP)

    def group(self, offset):
        return {"ep": self.z * GROUP + self.mate(offset)}

    def barrier(self):
        semaphore = pltpu.get_barrier_semaphore()
        for o in range(1, RING):
            pl.semaphore_signal(semaphore, inc=1, device_id=self.ring(o), device_id_type=MESH)
        for o in range(1, GROUP):
            pl.semaphore_signal(semaphore, inc=1, device_id=self.group(o), device_id_type=MESH)
        pl.semaphore_wait(semaphore, RING + GROUP - 2)


def remote(src, dst, send_sem, recv_sem, device):
    return pltpu.make_async_remote_copy(
        src_ref=src, dst_ref=dst, send_sem=send_sem, recv_sem=recv_sem,
        device_id=device, device_id_type=MESH,
    )


def slot_rows(ids_t, gates_t):
    experts = lax.broadcasted_iota(jnp.int32, (RING * GROUP, ROWS), 0)
    chosen = jnp.zeros((RING * GROUP, ROWS), F32)
    for k in range(TOP):
        chosen = chosen + jnp.where(ids_t[k : k + 1, :] == experts, 1.0, 0.0)
    before = lax.broadcasted_iota(jnp.int32, (ROWS, ROWS), 0) < lax.broadcasted_iota(
        jnp.int32, (ROWS, ROWS), 1
    )
    earlier = jnp.dot(
        chosen.astype(BF16), jnp.where(before, 1.0, 0.0).astype(BF16), preferred_element_type=F32
    )
    table = []
    for k in range(TOP):
        ids = ids_t[k : k + 1, :]
        rank = jnp.sum(jnp.where(ids == experts, earlier, 0.0), axis=0, keepdims=True)
        table.append(jnp.where(rank < CAP, ids.astype(F32) * CAP + rank, -1.0))
    table.append(jnp.full((2, ROWS), -1.0, F32))
    return jnp.concatenate(table + [gates_t], axis=0)


def row_slots(z, half):
    r = lax.broadcasted_iota(jnp.int32, (256, ROWS), 0)
    dest = jnp.zeros((256, ROWS), jnp.int32)
    for m in range(1, GROUP):
        dest = dest + jnp.where(r >= PAIR * m, 1, 0)
    within = r - PAIR * dest
    slot = within - CAP * half
    mine = (slot >= 0) & (slot < CAP) & (r < BLOCK)
    return jnp.where(mine, (z * GROUP + dest) * CAP + slot, -7).astype(F32)


def build_picks(z, tab, p, pick, pick_t, gate_hi, gate_lo, gate_hi_t, gate_lo_t):
    for half in range(2):
        slots = row_slots(z, half)
        ones = jnp.zeros((256, ROWS), F32)
        gates = jnp.zeros((256, ROWS), F32)
        for k in range(TOP):
            hit = tab[2 * p + half, k : k + 1, :] == slots
            ones = jnp.where(hit, 1.0, ones)
            gates = jnp.where(hit, tab[2 * p + half, 8 + k : 9 + k, :], gates)
        hi = gates.astype(BF16).astype(F32)
        lo = gates - hi
        lanes = slice(ROWS * half, ROWS * half + ROWS)
        pick[p, :, lanes] = ones.astype(BF16)
        gate_hi[p, :, lanes] = hi.astype(BF16)
        gate_lo[p, :, lanes] = lo.astype(BF16)
        pick_t[p, lanes, :] = ones.T.astype(BF16)
        gate_hi_t[p, lanes, :] = hi.T.astype(BF16)
        gate_lo_t[p, lanes, :] = lo.T.astype(BF16)


def dispatch(at, rows, zbuf, gbuf, xrecv, sems, before_gather, selectors, experts_of):
    zs, zr, xs, xr = sems

    def up_to(s):
        return (s, 0) if s < 4 else (3, ROWS)

    def plus(s, c):
        src = rows if s == 1 else zbuf.at[s - 1, pl.ds(0, ROWS)]
        p, r = up_to(s)
        return remote(src.at[:, cols(c)], zbuf.at[p, pl.ds(r, ROWS), cols(c)],
                      zs.at[0, s - 1, c], zr.at[0, s - 1, c], at.ring(1))

    def minus(s, c):
        src = rows if s == 1 else zbuf.at[s - 2, pl.ds(ROWS, ROWS)]
        return remote(src.at[:, cols(c)], zbuf.at[s - 1, pl.ds(ROWS, ROWS), cols(c)],
                      zs.at[1, s - 1, c], zr.at[1, s - 1, c], at.ring(-1))

    def has_plus(s, c):
        return s < 4 or (s == 4 and c < 2)

    def has_minus(s, c):
        return s < 4 or (s == 4 and c >= 2)

    for c in range(4):
        plus(1, c).start()
        minus(1, c).start()
    zbuf[0, 0:ROWS, :] = rows[...]
    before_gather()
    for s in range(1, 5):
        p = s - 1
        for c in (0, 1, 2, 3) if s < 4 else (0, 2, 1, 3):
            if has_plus(s, c):
                plus(s, c).wait_recv()
            if has_minus(s, c):
                minus(s, c).wait_recv()
            if s < 4:
                if has_plus(s + 1, c):
                    plus(s + 1, c).start()
                if has_minus(s + 1, c):
                    minus(s + 1, c).start()
            block = zbuf[p, :, c * CHUNK : (c + 1) * CHUNK]
            picked = jnp.zeros((BLOCK, CHUNK), F32)
            for selector in selectors:
                picked = picked + jnp.dot(selector[p, 0:BLOCK, :], block, preferred_element_type=F32)
            gbuf[p, :, :, c * CHUNK : (c + 1) * CHUNK] = picked.astype(BF16).reshape(
                GROUP, PAIR, CHUNK
            )
            for o in range(1, GROUP):
                remote(gbuf.at[p, at.mate(o), :, cols(c)], xrecv.at[p, at.g, :, cols(c)],
                       xs.at[p], xr.at[p], at.group(o)).start()
        xrecv[p, at.g] = gbuf[p, at.g]
        if s >= 2:
            arrive(at, p - 1, gbuf, xrecv, xs, xr)
            experts_of(p - 1)
    arrive(at, 3, gbuf, xrecv, xs, xr)
    for s in range(1, 5):
        for c in range(4):
            if has_plus(s, c):
                plus(s, c).wait_send()
            if has_minus(s, c):
                minus(s, c).wait_send()


def arrive(at, p, gbuf, xrecv, xs, xr):
    whole = remote(gbuf.at[p, pl.ds(0, GROUP - 1)], xrecv.at[p, pl.ds(0, GROUP - 1)],
                   xs.at[p], xr.at[p], at.group(1))
    whole.wait_send()
    whole.wait_recv()


def send_back(at, p, ybuf, crecv, cs, cr):
    for c in (0, 2, 1, 3):
        for o in range(1, GROUP):
            remote(ybuf.at[p, at.mate(o), :, cols(c)], crecv.at[p, at.g, :, cols(c)],
                   cs.at[p, c], cr.at[p, c], at.group(o)).start()
    crecv[p, at.g] = ybuf[p, at.g]


def combine(at, ybuf, crecv, rsend, rrecv, sems, selectors_t, finish):
    cs, cr, rs, rr = sems
    seen = set()

    def partial(p, half, c):
        if (p, c) not in seen:
            seen.add((p, c))
            whole = remote(ybuf.at[p, pl.ds(0, GROUP - 1), :, cols(c)],
                           crecv.at[p, pl.ds(0, GROUP - 1), :, cols(c)],
                           cs.at[p, c], cr.at[p, c], at.group(1))
            whole.wait_send()
            whole.wait_recv()
        block = crecv[p, :, :, c * CHUNK : (c + 1) * CHUNK].reshape(BLOCK, CHUNK)
        total = jnp.zeros((ROWS, CHUNK), F32)
        for selector in selectors_t:
            total = total + jnp.dot(
                selector[p, half * ROWS : (half + 1) * ROWS, 0:BLOCK], block,
                preferred_element_type=F32,
            )
        return total

    def has(way, t, c):
        return t > 1 or (c < 2) == (way == 0)

    def hop(way, t, c):
        return remote(rsend.at[way, t - 1, :, cols(c)], rrecv.at[way, t - 1, :, cols(c)],
                      rs.at[way, t - 1, c], rr.at[way, t - 1, c], at.ring(1 if way == 0 else -1))

    def unit(way, t, c):
        if not has(way, t, c):
            return
        p, half = (4 - t, 1) if way == 0 or t == 1 else (5 - t, 0)
        total = partial(p, half, c)
        window = slice(c * CHUNK, (c + 1) * CHUNK)
        if t > 1 and has(way, t - 1, c):
            hop(way, t - 1, c).wait_recv()
            total = total + rrecv[way, t - 2, :, window].astype(F32)
        rsend[way, t - 1, :, window] = total.astype(BF16)
        hop(way, t, c).start()

    for t in range(1, 5):
        for c in range(4):
            unit(0, t, c if t == 1 else c ^ 2)
            unit(1, t, c)
    for c in range(4):
        total = partial(0, 0, c)
        window = slice(c * CHUNK, (c + 1) * CHUNK)
        for way in range(2):
            hop(way, 4, c).wait_recv()
            total = total + rrecv[way, 3, :, window].astype(F32)
        finish(c, total)
    for t in range(1, 5):
        for c in range(4):
            for way in range(2):
                if has(way, t, c):
                    hop(way, t, c).wait_send()


def forward_kernel(rows, ids_t, gates_t, wg_hbm, wu_hbm, wd_hbm,
                   mixed, tab_out, pick_out, pick_t_out, hi_out, lo_out, gate_out, up_out, back_out,
                   wg, wu, wd, tab, tab_own, pick, pick_t, gate_hi, gate_lo, gate_hi_t, gate_lo_t,
                   zbuf, gbuf, xrecv, hidden, gate_pre, up_pre, ybuf, crecv, rsend, rrecv,
                   zs, zr, xs, xr, cs, cr, rs, rr, ts, tr, ws, os):
    at = Place()
    loads = [pltpu.make_async_copy(a.at[0], b, ws.at[i])
             for i, (a, b) in enumerate(((wg_hbm, wg), (wu_hbm, wu), (wd_hbm, wd)))]
    for load in loads:
        load.start()
    at.barrier()

    def tables():
        tab_own[...] = slot_rows(ids_t[...], gates_t[...])
        tab[0] = tab_own[...]
        sends = [remote(tab_own, tab.at[PLACE[RING - o]], ts.at[o], tr.at[PLACE[RING - o]],
                        at.ring(o)) for o in range(1, RING)]
        for send in sends:
            send.start()
        for send in sends:
            send.wait_recv()
        for p in range(4):
            build_picks(at.z, tab, p, pick, pick_t, gate_hi, gate_lo, gate_hi_t, gate_lo_t)
        for send in sends:
            send.wait_send()

    first = []

    def experts_of(p):
        if not first:
            first.append(1)
            for load in loads:
                load.wait()

        def up_step(n, carry):
            window = pl.ds(pl.multiple_of(n * 256, 256), 256)
            x = xrecv[p].reshape(BLOCK, D)
            a = jnp.dot(x, wg[:, window], preferred_element_type=F32)
            b = jnp.dot(x, wu[:, window], preferred_element_type=F32)
            gate_pre[p, :, window] = a
            up_pre[p, :, window] = b
            hidden[:, window] = (a * jax.nn.sigmoid(a) * b).astype(BF16)
            return carry

        lax.fori_loop(0, FFW // 256, up_step, 0)

        def down_step(n, carry):
            window = pl.ds(pl.multiple_of(n * 256, 256), 256)
            y = jnp.dot(hidden[...], wd[:, window], preferred_element_type=F32)
            ybuf[p, :, :, window] = y.astype(BF16).reshape(GROUP, PAIR, 256)
            return carry

        lax.fori_loop(0, D // 256, down_step, 0)

    dispatch(at, rows, zbuf, gbuf, xrecv, (zs, zr, xs, xr), tables, (pick,), experts_of)
    send_back(at, 2, ybuf, crecv, cs, cr)
    experts_of(3)
    for p in (3, 1, 0):
        send_back(at, p, ybuf, crecv, cs, cr)

    def finish(c, total):
        mixed[:, c * CHUNK : (c + 1) * CHUNK] = total

    combine(at, ybuf, crecv, rsend, rrecv, (cs, cr, rs, rr), (gate_hi_t, gate_lo_t), finish)
    outs = [pltpu.make_async_copy(a, b, os.at[i]) for i, (a, b) in enumerate((
        (tab, tab_out), (pick, pick_out), (pick_t, pick_t_out), (gate_hi, hi_out), (gate_lo, lo_out),
        (gate_pre, gate_out), (up_pre, up_out), (crecv, back_out)))]
    for out in outs:
        out.start()
    for out in outs:
        out.wait()


def backward_kernel(rows, state_grad, tab_hbm, pick_hbm, pick_t_hbm, hi_hbm, lo_hbm, gate_hbm, up_hbm,
                    back_hbm, wg_hbm, wu_hbm, wd_hbm,
                    grad_in, gates_out,
                    wg, wu, wd, tab, pick, pick_t, gate_hi, gate_lo, gate_pre, up_pre, back,
                    zbuf, gbuf, xrecv, hidden, hidden2, ybuf, crecv, rsend, rrecv, dots, dots_recv,
                    zs, zr, xs, xr, cs, cr, rs, rr, ds, dr, ws):
    at = Place()
    loads = [pltpu.make_async_copy(a, b, ws.at[i]) for i, (a, b) in enumerate((
        (tab_hbm, tab), (pick_hbm, pick), (pick_t_hbm, pick_t), (hi_hbm, gate_hi), (lo_hbm, gate_lo),
        (wd_hbm.at[0], wd), (gate_hbm, gate_pre), (up_hbm, up_pre), (wg_hbm.at[0], wg),
        (wu_hbm.at[0], wu), (back_hbm, back)))]
    for load in loads:
        load.start()
    at.barrier()

    def tables():
        for load in loads[:5]:
            load.wait()

    first = []

    def experts_of(p):
        if not first:
            first.append(1)
            for load in loads[5:]:
                load.wait()
        across = (((1,), (1,)), ((), ()))

        def down_step(n, carry):
            window = pl.ds(pl.multiple_of(n * 256, 256), 256)
            x = xrecv[p].reshape(BLOCK, D)
            grad = lax.dot_general(x, wd[window, :], across, preferred_element_type=F32)
            a = gate_pre[p, :, window]
            s = jax.nn.sigmoid(a)
            hidden[:, window] = (grad * up_pre[p, :, window] * (s * (1.0 + a * (1.0 - s)))).astype(BF16)
            hidden2[:, window] = (grad * (a * s)).astype(BF16)
            return carry

        lax.fori_loop(0, FFW // 256, down_step, 0)

        def up_step(n, carry):
            window = pl.ds(pl.multiple_of(n * 256, 256), 256)
            y = lax.dot_general(hidden[...], wg[window, :], across, preferred_element_type=F32)
            y = y + lax.dot_general(hidden2[...], wu[window, :], across, preferred_element_type=F32)
            ybuf[p, :, :, window] = y.astype(BF16).reshape(GROUP, PAIR, 256)
            return carry

        lax.fori_loop(0, D // 256, up_step, 0)

    def gate_dots(p):
        products = lax.dot_general(back[p].reshape(BLOCK, D), zbuf[p], (((1,), (1,)), ((), ())),
                                   preferred_element_type=F32)
        for half in range(2):
            slots = row_slots(at.z, half)[0:BLOCK]
            mine = products[:, ROWS * half : ROWS * half + ROWS]
            picked = [jnp.sum(jnp.where(tab[2 * p + half, k : k + 1, :] == slots, mine, 0.0),
                              axis=0, keepdims=True) for k in range(TOP)]
            dots[2 * p + half] = jnp.concatenate(picked + [jnp.zeros((2, ROWS), F32)], axis=0)

    dispatch(at, rows, zbuf, gbuf, xrecv, (zs, zr, xs, xr), tables, (gate_hi, gate_lo), experts_of)
    send_back(at, 2, ybuf, crecv, cs, cr)
    experts_of(3)
    for p in (3, 1, 0):
        send_back(at, p, ybuf, crecv, cs, cr)
    for p in range(4):
        gate_dots(p)
    dot_sends = [remote(dots.at[PLACE[o]], dots_recv.at[PLACE[RING - o]], ds.at[o],
                        dr.at[PLACE[RING - o]], at.ring(o)) for o in range(1, RING)]
    for send in dot_sends:
        send.start()

    def finish(c, total):
        window = slice(c * CHUNK, (c + 1) * CHUNK)
        grad_in[:, window] = (state_grad[:, window] + total).astype(BF16)

    combine(at, ybuf, crecv, rsend, rrecv, (cs, cr, rs, rr), (pick_t,), finish)
    total = dots[0]
    for o in range(1, RING):
        dot_sends[o - 1].wait_recv()
    for o in range(1, RING):
        total = total + dots_recv[PLACE[RING - o]]
    gates_out[...] = total
    for send in dot_sends:
        send.wait_send()


VMEM = pl.BlockSpec(memory_space=pltpu.VMEM)
ANY = pl.BlockSpec(memory_space=pl.ANY)
DMA = pltpu.SemaphoreType.DMA
SELECTOR = ((4, 256, 256), BF16)
PAIRS = ((4, GROUP, PAIR, D), BF16)
PRES = ((4, BLOCK, FFW), F32)
TABLES = ((RING, 16, ROWS), F32)


def exchange_scratch():
    return dict(
        zbuf=pltpu.VMEM((4, 2 * ROWS, D), BF16), gbuf=pltpu.VMEM(*PAIRS), xrecv=pltpu.VMEM(*PAIRS),
        ybuf=pltpu.VMEM(*PAIRS), crecv=pltpu.VMEM(*PAIRS),
        rsend=pltpu.VMEM((2, 4, ROWS, D), BF16), rrecv=pltpu.VMEM((2, 4, ROWS, D), BF16),
        wg=pltpu.VMEM((D, FFW), BF16), wu=pltpu.VMEM((D, FFW), BF16), wd=pltpu.VMEM((FFW, D), BF16),
        zs=DMA((2, 4, 4)), zr=DMA((2, 4, 4)), xs=DMA((4,)), xr=DMA((4,)), cs=DMA((4, 4)), cr=DMA((4, 4)),
        rs=DMA((2, 4, 4)), rr=DMA((2, 4, 4)),
    )


def run_forward(rows, ids_t, gates_t, wg, wu, wd):
    s = exchange_scratch()
    selector = pltpu.VMEM(*SELECTOR)
    outs = [((ROWS, D), F32), TABLES, SELECTOR, SELECTOR, SELECTOR, SELECTOR, PRES, PRES, PAIRS]
    return pl.pallas_call(
        forward_kernel,
        out_shape=[jax.ShapeDtypeStruct(*o) for o in outs],
        in_specs=[VMEM, VMEM, VMEM, ANY, ANY, ANY],
        out_specs=[VMEM] + [ANY] * 8,
        scratch_shapes=[
            s["wg"], s["wu"], s["wd"], pltpu.VMEM(*TABLES), pltpu.VMEM((16, ROWS), F32),
            selector, selector, selector, selector, selector, selector,
            s["zbuf"], s["gbuf"], s["xrecv"], pltpu.VMEM((BLOCK, FFW), BF16),
            pltpu.VMEM(*PRES), pltpu.VMEM(*PRES), s["ybuf"], s["crecv"], s["rsend"], s["rrecv"],
            s["zs"], s["zr"], s["xs"], s["xr"], s["cs"], s["cr"], s["rs"], s["rr"],
            DMA((RING,)), DMA((RING,)), DMA((3,)), DMA((8,)),
        ],
        compiler_params=pltpu.CompilerParams(
            collective_id=0, has_side_effects=True, vmem_limit_bytes=64 * 1024 * 1024 - 65536
        ),
        name="forward_exchange",
    )(rows, ids_t, gates_t, wg, wu, wd)


def run_backward(rows, state_grad, saved, wg, wu, wd):
    s = exchange_scratch()
    selector = pltpu.VMEM(*SELECTOR)
    return pl.pallas_call(
        backward_kernel,
        out_shape=[jax.ShapeDtypeStruct((ROWS, D), BF16), jax.ShapeDtypeStruct((8, ROWS), F32)],
        in_specs=[VMEM, VMEM] + [ANY] * 11,
        out_specs=[VMEM, VMEM],
        scratch_shapes=[
            s["wg"], s["wu"], s["wd"], pltpu.VMEM(*TABLES), selector, selector, selector, selector,
            pltpu.VMEM(*PRES), pltpu.VMEM(*PRES), pltpu.VMEM(*PAIRS),
            s["zbuf"], s["gbuf"], s["xrecv"], pltpu.VMEM((BLOCK, FFW), BF16), pltpu.VMEM((BLOCK, FFW), BF16),
            s["ybuf"], s["crecv"], s["rsend"], s["rrecv"],
            pltpu.VMEM((RING, 8, ROWS), F32), pltpu.VMEM((RING, 8, ROWS), F32),
            s["zs"], s["zr"], s["xs"], s["xr"], s["cs"], s["cr"], s["rs"], s["rr"],
            DMA((RING,)), DMA((RING,)), DMA((11,)),
        ],
        compiler_params=pltpu.CompilerParams(
            collective_id=1, has_side_effects=True, vmem_limit_bytes=64 * 1024 * 1024 - 65536
        ),
        name="backward_exchange",
    )(rows, state_grad, *saved, wg, wu, wd)


def from_behind(block, axis, distance):
    devices = range(lax.axis_size(axis))
    route = [(i - distance, i) for i in devices if i - distance in devices]
    return lax.ppermute(block, axis, route)


def foot_term(horizon, contact_rep, velocity):
    return foot_weight * horizon[:, None] * contact_rep * velocity


def per_device(
    frames_in,
    expert_ids,
    gate_values,
    gate_weight,
    up_weight,
    down_weight,
    norm_gain,
    pose_weight,
    target_pose,
    foot_contact,
):
    tok_rows, model_width = frames_in.shape
    ep_count = lax.axis_size("ep")
    ids_t = jnp.pad(expert_ids.T, ((0, 2), (0, 0)), constant_values=-1)
    gates_t = jnp.pad(gate_values.T, ((0, 2), (0, 0)))
    mixed_rows, *saved = run_forward(frames_in, ids_t, gates_t, gate_weight, up_weight, down_weight)
    state_rows = frames_in.astype(jnp.float32) + mixed_rows
    inverse_rms = lax.rsqrt(jnp.mean(state_rows * state_rows, axis=1, keepdims=True) + epsilon)
    unit_rows = state_rows * inverse_rms
    normed = (unit_rows * norm_gain).astype(jnp.bfloat16)
    pose_out = jnp.dot(normed, pose_weight, preferred_element_type=jnp.float32)
    pose_cols = pose_out.shape[1]
    device = lax.axis_index("seg") * ep_count + lax.axis_index("ep")
    frames_all = lax.axis_size("seg") * ep_count * tok_rows
    frame_index = device * tok_rows + jnp.arange(tok_rows, dtype=jnp.int32)
    horizon = 0.5 + frame_index.astype(jnp.float32) / (frames_all - 1)
    feet_count = foot_contact.shape[1]
    foot_cols = 3 * feet_count
    foot_pos = pose_out[:, :foot_cols]
    contact_float = foot_contact.astype(jnp.float32)
    contact_rep = jnp.repeat(contact_float, 3, axis=1)
    before = from_behind(foot_pos[tok_rows - 1 :], ("seg", "ep"), 1)
    earlier = jnp.concatenate([before, foot_pos[:-1]], 0)
    velocity = jnp.where((frame_index > 0)[:, None], foot_pos - earlier, 0.0)
    foot_pull = foot_term(horizon, contact_rep, velocity)
    next_pull = from_behind(foot_pull[:1], ("seg", "ep"), -1)
    pose_error = pose_out - target_pose
    local_sum = 0.5 * jnp.sum(horizon[:, None] * pose_error * pose_error) + 0.5 * jnp.sum(
        foot_pull * velocity
    )
    summed = lax.psum(local_sum, ("seg", "ep"))
    loss_value = summed / (frames_all * pose_cols)
    later_pull = jnp.concatenate([foot_pull[1:], next_pull], 0)
    grad_pose = horizon[:, None] * pose_error
    grad_pose = jnp.concatenate(
        [grad_pose[:, :foot_cols] + (foot_pull - later_pull), grad_pose[:, foot_cols:]], 1
    )
    grad_normed = jnp.einsum(
        "tp,dp->td", grad_pose.astype(jnp.bfloat16), pose_weight, preferred_element_type=jnp.float32
    )
    scaled = grad_normed * norm_gain
    grad_state = inverse_rms * (
        scaled - unit_rows * jnp.mean(scaled * unit_rows, axis=1, keepdims=True)
    )
    moe_grad = grad_state.astype(jnp.bfloat16)
    grad_input, grad_gates_t = run_backward(
        moe_grad, grad_state, saved, gate_weight, up_weight, down_weight
    )
    return (grad_input, grad_gates_t[: expert_ids.shape[1]].T, loss_value)


def solution(mesh):
    in_specs = (
        P(("seg", "ep"), None),
        P(("seg", "ep"), None),
        P(("seg", "ep"), None),
        P("ep", None, None),
        P("ep", None, None),
        P("ep", None, None),
        P(),
        P(),
        P(("seg", "ep"), None),
        P(("seg", "ep"), None),
    )
    out_specs = (P(("seg", "ep"), None), P(("seg", "ep"), None), P())
    return jax.shard_map(
        per_device, mesh=mesh, in_specs=in_specs, out_specs=out_specs, check_vma=False
    )
```

```python
import jax
import jax.numpy as jnp
from jax import lax
from jax.experimental import pallas as pl
from jax.experimental.pallas import tpu as pltpu
from jax.sharding import PartitionSpec as P

MESH = pl.DeviceIdType.MESH
epsilon = 1e-06
foot_weight = 2.0

RING = 8
GROUP = 8
ROWS = 128
CAP = 12
TOP = 6
D = 2048
POSE = 256
FEET = 4
FFW = 768
CHUNK = 512
PAIR = 2 * CAP
BLOCK = GROUP * PAIR
F32 = jnp.float32
BF16 = jnp.bfloat16

PLACE = {0: 0, 1: 1, 7: 2, 2: 3, 6: 4, 3: 5, 5: 6, 4: 7}


def cols(c):
    return pl.ds(c * CHUNK, CHUNK)


class Place:
    def __init__(self):
        ep = lax.axis_index("ep")
        self.z = lax.div(ep, GROUP)
        self.g = lax.rem(ep, GROUP)
        self.seg = lax.axis_index("seg")
        self.segs = lax.axis_size("seg")
        self.index = self.seg * (RING * GROUP) + ep

    def ring(self, distance):
        return {"ep": lax.rem(self.z + distance + RING, RING) * GROUP + self.g}

    def mate(self, offset):
        return lax.rem(self.g + offset, GROUP)

    def group(self, offset):
        return {"ep": self.z * GROUP + self.mate(offset)}

    def segment(self, offset):
        return {"seg": lax.rem(self.seg + offset, self.segs)}

    def next(self, offset):
        devices = RING * GROUP * self.segs
        index = lax.rem(self.index + offset + devices, devices)
        return {"seg": lax.div(index, RING * GROUP), "ep": lax.rem(index, RING * GROUP)}

    def barrier(self):
        semaphore = pltpu.get_barrier_semaphore()
        for o in range(1, RING):
            pl.semaphore_signal(semaphore, inc=1, device_id=self.ring(o), device_id_type=MESH)
        for o in range(1, GROUP):
            pl.semaphore_signal(semaphore, inc=1, device_id=self.group(o), device_id_type=MESH)
        for o in range(1, self.segs):
            pl.semaphore_signal(semaphore, inc=1, device_id=self.segment(o), device_id_type=MESH)
        for o in (-1, 1):
            pl.semaphore_signal(semaphore, inc=1, device_id=self.next(o), device_id_type=MESH)
        pl.semaphore_wait(semaphore, RING + GROUP + self.segs - 1)


def remote(src, dst, send_sem, recv_sem, device):
    return pltpu.make_async_remote_copy(
        src_ref=src, dst_ref=dst, send_sem=send_sem, recv_sem=recv_sem,
        device_id=device, device_id_type=MESH,
    )


def slot_rows(ids_t, gates_t):
    experts = lax.broadcasted_iota(jnp.int32, (RING * GROUP, ROWS), 0)
    chosen = jnp.zeros((RING * GROUP, ROWS), F32)
    for k in range(TOP):
        chosen = chosen + jnp.where(ids_t[k : k + 1, :] == experts, 1.0, 0.0)
    before = lax.broadcasted_iota(jnp.int32, (ROWS, ROWS), 0) < lax.broadcasted_iota(
        jnp.int32, (ROWS, ROWS), 1
    )
    earlier = jnp.dot(
        chosen.astype(BF16), jnp.where(before, 1.0, 0.0).astype(BF16), preferred_element_type=F32
    )
    table = []
    for k in range(TOP):
        ids = ids_t[k : k + 1, :]
        rank = jnp.sum(jnp.where(ids == experts, earlier, 0.0), axis=0, keepdims=True)
        table.append(jnp.where(rank < CAP, ids.astype(F32) * CAP + rank, -1.0))
    table.append(jnp.full((2, ROWS), -1.0, F32))
    return jnp.concatenate(table + [gates_t], axis=0)


def row_slots(z, half):
    r = lax.broadcasted_iota(jnp.int32, (256, ROWS), 0)
    dest = jnp.zeros((256, ROWS), jnp.int32)
    for m in range(1, GROUP):
        dest = dest + jnp.where(r >= PAIR * m, 1, 0)
    within = r - PAIR * dest
    slot = within - CAP * half
    mine = (slot >= 0) & (slot < CAP) & (r < BLOCK)
    return jnp.where(mine, (z * GROUP + dest) * CAP + slot, -7).astype(F32)


def build_picks(z, tab, p, pick, pick_t, gate_hi, gate_lo, gate_hi_t, gate_lo_t):
    for half in range(2):
        slots = row_slots(z, half)
        ones = jnp.zeros((256, ROWS), F32)
        gates = jnp.zeros((256, ROWS), F32)
        for k in range(TOP):
            hit = tab[2 * p + half, k : k + 1, :] == slots
            ones = jnp.where(hit, 1.0, ones)
            gates = jnp.where(hit, tab[2 * p + half, 8 + k : 9 + k, :], gates)
        hi = gates.astype(BF16).astype(F32)
        lo = gates - hi
        lanes = slice(ROWS * half, ROWS * half + ROWS)
        pick[p, :, lanes] = ones.astype(BF16)
        gate_hi[p, :, lanes] = hi.astype(BF16)
        gate_lo[p, :, lanes] = lo.astype(BF16)
        pick_t[p, lanes, :] = ones.T.astype(BF16)
        gate_hi_t[p, lanes, :] = hi.T.astype(BF16)
        gate_lo_t[p, lanes, :] = lo.T.astype(BF16)


def dispatch(at, rows, zbuf, gbuf, xrecv, sems, before_gather, selectors, experts_of):
    zs, zr, xs, xr = sems

    def up_to(s):
        return (s, 0) if s < 4 else (3, ROWS)

    def plus(s, c):
        src = rows if s == 1 else zbuf.at[s - 1, pl.ds(0, ROWS)]
        p, r = up_to(s)
        return remote(src.at[:, cols(c)], zbuf.at[p, pl.ds(r, ROWS), cols(c)],
                      zs.at[0, s - 1, c], zr.at[0, s - 1, c], at.ring(1))

    def minus(s, c):
        src = rows if s == 1 else zbuf.at[s - 2, pl.ds(ROWS, ROWS)]
        return remote(src.at[:, cols(c)], zbuf.at[s - 1, pl.ds(ROWS, ROWS), cols(c)],
                      zs.at[1, s - 1, c], zr.at[1, s - 1, c], at.ring(-1))

    def has_plus(s, c):
        return s < 4 or (s == 4 and c < 2)

    def has_minus(s, c):
        return s < 4 or (s == 4 and c >= 2)

    for c in range(4):
        plus(1, c).start()
        minus(1, c).start()
    zbuf[0, 0:ROWS, :] = rows[...]
    before_gather()
    for s in range(1, 5):
        p = s - 1
        for c in (0, 1, 2, 3) if s < 4 else (0, 2, 1, 3):
            if has_plus(s, c):
                plus(s, c).wait_recv()
            if has_minus(s, c):
                minus(s, c).wait_recv()
            if s < 4:
                if has_plus(s + 1, c):
                    plus(s + 1, c).start()
                if has_minus(s + 1, c):
                    minus(s + 1, c).start()
            block = zbuf[p, :, c * CHUNK : (c + 1) * CHUNK]
            picked = jnp.zeros((BLOCK, CHUNK), F32)
            for selector in selectors:
                picked = picked + jnp.dot(selector[p, 0:BLOCK, :], block, preferred_element_type=F32)
            gbuf[p, :, :, c * CHUNK : (c + 1) * CHUNK] = picked.astype(BF16).reshape(
                GROUP, PAIR, CHUNK
            )
            for o in range(1, GROUP):
                remote(gbuf.at[p, at.mate(o), :, cols(c)], xrecv.at[p, at.g, :, cols(c)],
                       xs.at[p], xr.at[p], at.group(o)).start()
        xrecv[p, at.g] = gbuf[p, at.g]
        if s >= 2:
            arrive(at, p - 1, gbuf, xrecv, xs, xr)
            experts_of(p - 1)
    arrive(at, 3, gbuf, xrecv, xs, xr)
    for s in range(1, 5):
        for c in range(4):
            if has_plus(s, c):
                plus(s, c).wait_send()
            if has_minus(s, c):
                minus(s, c).wait_send()


def arrive(at, p, gbuf, xrecv, xs, xr):
    whole = remote(gbuf.at[p, pl.ds(0, GROUP - 1)], xrecv.at[p, pl.ds(0, GROUP - 1)],
                   xs.at[p], xr.at[p], at.group(1))
    whole.wait_send()
    whole.wait_recv()


def send_back(at, p, ybuf, crecv, cs, cr):
    for c in (0, 2, 1, 3):
        for o in range(1, GROUP):
            remote(ybuf.at[p, at.mate(o), :, cols(c)], crecv.at[p, at.g, :, cols(c)],
                   cs.at[p, c], cr.at[p, c], at.group(o)).start()
    crecv[p, at.g] = ybuf[p, at.g]


def combine(at, ybuf, crecv, rsend, rrecv, sems, selectors_t, finish):
    cs, cr, rs, rr = sems
    seen = set()

    def partial(p, half, c):
        if (p, c) not in seen:
            seen.add((p, c))
            whole = remote(ybuf.at[p, pl.ds(0, GROUP - 1), :, cols(c)],
                           crecv.at[p, pl.ds(0, GROUP - 1), :, cols(c)],
                           cs.at[p, c], cr.at[p, c], at.group(1))
            whole.wait_send()
            whole.wait_recv()
        block = crecv[p, :, :, c * CHUNK : (c + 1) * CHUNK].reshape(BLOCK, CHUNK)
        total = jnp.zeros((ROWS, CHUNK), F32)
        for selector in selectors_t:
            total = total + jnp.dot(
                selector[p, half * ROWS : (half + 1) * ROWS, 0:BLOCK], block,
                preferred_element_type=F32,
            )
        return total

    def has(way, t, c):
        return t > 1 or (c < 2) == (way == 0)

    def hop(way, t, c):
        return remote(rsend.at[way, t - 1, :, cols(c)], rrecv.at[way, t - 1, :, cols(c)],
                      rs.at[way, t - 1, c], rr.at[way, t - 1, c], at.ring(1 if way == 0 else -1))

    def unit(way, t, c):
        if not has(way, t, c):
            return
        p, half = (4 - t, 1) if way == 0 or t == 1 else (5 - t, 0)
        total = partial(p, half, c)
        window = slice(c * CHUNK, (c + 1) * CHUNK)
        if t > 1 and has(way, t - 1, c):
            hop(way, t - 1, c).wait_recv()
            total = total + rrecv[way, t - 2, :, window].astype(F32)
        rsend[way, t - 1, :, window] = total.astype(BF16)
        hop(way, t, c).start()

    for t in range(1, 5):
        for c in range(4):
            unit(0, t, c if t == 1 else c ^ 2)
            unit(1, t, c)
    for c in range(4):
        total = partial(0, 0, c)
        window = slice(c * CHUNK, (c + 1) * CHUNK)
        for way in range(2):
            hop(way, 4, c).wait_recv()
            total = total + rrecv[way, 3, :, window].astype(F32)
        finish(c, total)
    for t in range(1, 5):
        for c in range(4):
            for way in range(2):
                if has(way, t, c):
                    hop(way, t, c).wait_send()


def step_kernel(rows, ids, gates, wg_hbm, wu_hbm, wd_hbm, gain, pose_weight, target, contact,
                grad_in, gates_out, loss_out,
                wg, wu, wd, tab, tab_own, pick, pick_t, gate_hi, gate_lo, gate_hi_t, gate_lo_t,
                zbuf, gbuf, xrecv, hidden, hidden2, gate_pre, up_pre, ybuf, crecv, crecv2, rsend, rrecv,
                turn, state, grad_state, moe_grad, foot, foot_recv, tiles, dots, dots_recv,
                zs, zr, xs, xr, cs, cr, rs, rr, ts, tr, ws, fs, fr, ls, lr, ds, dr):
    at = Place()
    loads = [pltpu.make_async_copy(a.at[0], b, ws.at[i])
             for i, (a, b) in enumerate(((wg_hbm, wg), (wu_hbm, wu), (wd_hbm, wd)))]
    for load in loads:
        load.start()
    at.barrier()
    across = (((1,), (1,)), ((), ()))

    def tables():
        turn[...] = jnp.zeros((2, ROWS, ROWS), F32)
        turn[0, :, 0:TOP] = ids[...].astype(F32)
        turn[1, :, 0:TOP] = gates[...]
        tab_own[...] = slot_rows(turn[0].T[0:8], turn[1].T[0:8])
        tab[0] = tab_own[...]
        sends = [remote(tab_own, tab.at[PLACE[RING - o]], ts.at[o], tr.at[PLACE[RING - o]],
                        at.ring(o)) for o in range(1, RING)]
        for send in sends:
            send.start()
        for send in sends:
            send.wait_recv()
        for p in range(4):
            build_picks(at.z, tab, p, pick, pick_t, gate_hi, gate_lo, gate_hi_t, gate_lo_t)
        for send in sends:
            send.wait_send()

    first = []

    def experts_forward(p):
        if not first:
            first.append(1)
            for load in loads:
                load.wait()

        def up_step(n, carry):
            window = pl.ds(pl.multiple_of(n * 256, 256), 256)
            x = xrecv[p].reshape(BLOCK, D)
            a = jnp.dot(x, wg[:, window], preferred_element_type=F32)
            b = jnp.dot(x, wu[:, window], preferred_element_type=F32)
            gate_pre[p, :, window] = a
            up_pre[p, :, window] = b
            hidden[:, window] = (a * jax.nn.sigmoid(a) * b).astype(BF16)
            return carry

        lax.fori_loop(0, FFW // 256, up_step, 0)

        def down_step(n, carry):
            window = pl.ds(pl.multiple_of(n * 256, 256), 256)
            y = jnp.dot(hidden[...], wd[:, window], preferred_element_type=F32)
            ybuf[p, :, :, window] = y.astype(BF16).reshape(GROUP, PAIR, 256)
            return carry

        lax.fori_loop(0, D // 256, down_step, 0)

    dispatch(at, rows, zbuf, gbuf, xrecv, (zs, zr, xs, xr), tables, (pick,), experts_forward)
    send_back(at, 2, ybuf, crecv, cs, cr)
    experts_forward(3)
    for p in (3, 1, 0):
        send_back(at, p, ybuf, crecv, cs, cr)
    squares = []

    def finish_state(c, total):
        window = slice(c * CHUNK, (c + 1) * CHUNK)
        sums = rows[:, window].astype(F32) + total
        state[:, window] = sums
        squares.append(jnp.sum(sums * sums, axis=1, keepdims=True))

    combine(at, ybuf, crecv, rsend, rrecv, (cs, cr, rs, rr), (gate_hi_t, gate_lo_t), finish_state)

    inverse = lax.rsqrt((squares[0] + squares[1] + squares[2] + squares[3]) / D + epsilon)
    pose = jnp.zeros((ROWS, POSE), F32)
    for c in range(4):
        window = slice(c * CHUNK, (c + 1) * CHUNK)
        normed = (state[:, window] * inverse * gain[:, window]).astype(BF16)
        pose = pose + jnp.dot(normed, pose_weight[window, :], preferred_element_type=F32)
    place = pl.multiple_of(at.index * ROWS, ROWS)
    frames = lax.broadcasted_iota(jnp.int32, (ROWS, 1), 0) + place
    frames_all = RING * GROUP * ROWS * at.segs
    horizon = 0.5 + frames.astype(F32) / (frames_all - 1)
    lanes = lax.broadcasted_iota(jnp.int32, (ROWS, ROWS), 1)
    contacts = jnp.zeros((ROWS, ROWS), F32)
    for k in range(FEET):
        here = (lanes >= 3 * k) & (lanes < 3 * k + 3)
        contacts = jnp.where(here, contact[:, k : k + 1].astype(F32), contacts)
    feet = pose[:, 0:ROWS]
    foot[0:8, :] = feet[0:8]
    foot[8:16, :] = contacts[0:8]
    foot[16:24, :] = feet[ROWS - 8 :]
    to_next = remote(foot.at[pl.ds(16, 8)], foot_recv.at[pl.ds(16, 8)], fs.at[0], fr.at[0], at.next(1))
    to_last = remote(foot.at[pl.ds(0, 16)], foot_recv.at[pl.ds(0, 16)], fs.at[1], fr.at[1], at.next(-1))
    to_next.start()
    to_last.start()
    error = pose - target[...]
    grad_pose = horizon * error
    grad_far = grad_pose[:, ROWS:].astype(BF16)
    squared = grad_pose * error
    grad_parts = [
        lax.dot_general(grad_far, pose_weight[c * CHUNK : (c + 1) * CHUNK, ROWS:], across,
                        preferred_element_type=F32) for c in range(4)]
    for c in range(4):
        grad_state[:, c * CHUNK : (c + 1) * CHUNK] = grad_parts[c]
    to_next.wait_recv()
    to_last.wait_recv()
    row = lax.broadcasted_iota(jnp.int32, (ROWS, ROWS), 0)
    earlier = jnp.where(row == 0, foot_recv[23:24, :], pltpu.roll(feet, 1, 0))
    velocity = jnp.where(frames > 0, feet - earlier, 0.0)
    pull = foot_weight * horizon * contacts * velocity
    next_horizon = 0.5 + (place + ROWS).astype(F32) / (frames_all - 1)
    next_pull = foot_weight * next_horizon * foot_recv[8:9, :] * (foot_recv[0:1, :] - feet[ROWS - 1 :])
    next_pull = jnp.where(frames[ROWS - 1 :] < frames_all - 1, next_pull, 0.0)
    later = jnp.where(row == ROWS - 1, next_pull, pltpu.roll(pull, ROWS - 1, 0))
    terms = squared[:, 0:ROWS] + squared[:, ROWS:] + pull * velocity
    grad_near = (grad_pose[:, 0:ROWS] + (pull - later)).astype(BF16)
    products = jnp.zeros((ROWS, 1), F32)
    for c in range(4):
        window = slice(c * CHUNK, (c + 1) * CHUNK)
        grad_normed = grad_state[:, window] + lax.dot_general(
            grad_near, pose_weight[window, 0:ROWS], across, preferred_element_type=F32
        )
        scaled = grad_normed * gain[:, window]
        grad_state[:, window] = scaled
        products = products + jnp.sum(scaled * (state[:, window] * inverse), axis=1, keepdims=True)
    products = products / D
    for c in range(4):
        window = slice(c * CHUNK, (c + 1) * CHUNK)
        grads = inverse * (grad_state[:, window] - state[:, window] * inverse * products)
        grad_state[:, window] = grads
        moe_grad[:, window] = grads.astype(BF16)
    to_next.wait_send()
    to_last.wait_send()

    tile = jnp.zeros((8, ROWS), F32)
    for r in range(0, ROWS, 8):
        tile = tile + terms[r : r + 8]

    def share(stage, here, size, device, value):
        tiles[stage, here] = value
        sends = [remote(tiles.at[stage, here], tiles.at[stage, here], ls.at[stage, o], lr.at[stage],
                        device(o)) for o in range(1, size)]
        for send in sends:
            send.start()
        return sends

    def gather_tile(stage, size, sends):
        remote(tiles.at[stage, pl.ds(0, size - 1)], tiles.at[stage, pl.ds(0, size - 1)],
               ls.at[stage, 0], lr.at[stage], at.ring(1)).wait_recv()
        for send in sends:
            send.wait_send()
        total = tiles[stage, 0]
        for i in range(1, size):
            total = total + tiles[stage, i]
        return total

    shares = []

    def experts_backward(p):
        if p == 0:
            value = gather_tile(0, RING, shares.pop())
            shares.append(share(1, at.g, GROUP, at.group, value))
        if p == 1:
            value = gather_tile(1, GROUP, shares.pop())
            shares.append(share(2, at.seg, at.segs, at.segment, value))

        def down_step(n, carry):
            window = pl.ds(pl.multiple_of(n * 256, 256), 256)
            x = xrecv[p].reshape(BLOCK, D)
            grad = lax.dot_general(x, wd[window, :], across, preferred_element_type=F32)
            a = gate_pre[p, :, window]
            s = jax.nn.sigmoid(a)
            hidden[:, window] = (grad * up_pre[p, :, window] * (s * (1.0 + a * (1.0 - s)))).astype(BF16)
            hidden2[:, window] = (grad * (a * s)).astype(BF16)
            return carry

        lax.fori_loop(0, FFW // 256, down_step, 0)

        def up_step(n, carry):
            window = pl.ds(pl.multiple_of(n * 256, 256), 256)
            y = lax.dot_general(hidden[...], wg[window, :], across, preferred_element_type=F32)
            y = y + lax.dot_general(hidden2[...], wu[window, :], across, preferred_element_type=F32)
            ybuf[p, :, :, window] = y.astype(BF16).reshape(GROUP, PAIR, 256)
            return carry

        lax.fori_loop(0, D // 256, up_step, 0)

    def gate_dots(p):
        products = lax.dot_general(crecv[p].reshape(BLOCK, D), zbuf[p], across,
                                   preferred_element_type=F32)
        for half in range(2):
            slots = row_slots(at.z, half)[0:BLOCK]
            mine = products[:, ROWS * half : ROWS * half + ROWS]
            picked = [jnp.sum(jnp.where(tab[2 * p + half, k : k + 1, :] == slots, mine, 0.0),
                              axis=0, keepdims=True) for k in range(TOP)]
            dots[2 * p + half] = jnp.concatenate(picked + [jnp.zeros((2, ROWS), F32)], axis=0)

    def share_loss():
        shares.append(share(0, at.z, RING, at.ring, tile))

    dispatch(at, moe_grad, zbuf, gbuf, xrecv, (zs, zr, xs, xr), share_loss, (gate_hi, gate_lo),
             experts_backward)
    send_back(at, 2, ybuf, crecv2, cs, cr)
    experts_backward(3)
    for p in (3, 1, 0):
        send_back(at, p, ybuf, crecv2, cs, cr)
    for p in range(4):
        gate_dots(p)
    dot_sends = [remote(dots.at[PLACE[o]], dots_recv.at[PLACE[RING - o]], ds.at[o],
                        dr.at[PLACE[RING - o]], at.ring(o)) for o in range(1, RING)]
    for send in dot_sends:
        send.start()

    def finish_input(c, total):
        window = slice(c * CHUNK, (c + 1) * CHUNK)
        grad_in[:, window] = (grad_state[:, window] + total).astype(BF16)

    combine(at, ybuf, crecv2, rsend, rrecv, (cs, cr, rs, rr), (pick_t,), finish_input)
    loss = gather_tile(2, at.segs, shares.pop())
    loss_out[0, 0] = jnp.sum(loss) * (0.5 / (frames_all * POSE))
    for send in dot_sends:
        send.wait_recv()
    total = dots[0]
    for o in range(1, RING):
        total = total + dots_recv[PLACE[RING - o]]
    gates_out[...] = total
    for send in dot_sends:
        send.wait_send()


VMEM = pl.BlockSpec(memory_space=pltpu.VMEM)
SMEM = pl.BlockSpec(memory_space=pltpu.SMEM)
ANY = pl.BlockSpec(memory_space=pl.ANY)
DMA = pltpu.SemaphoreType.DMA


def per_device(
    frames_in,
    expert_ids,
    gate_values,
    gate_weight,
    up_weight,
    down_weight,
    norm_gain,
    pose_weight,
    target_pose,
    foot_contact,
):
    segs = lax.axis_size("seg")
    selector = pltpu.VMEM((4, 256, 256), BF16)
    pairs = pltpu.VMEM((4, GROUP, PAIR, D), BF16)
    hidden = pltpu.VMEM((BLOCK, FFW), BF16)
    pres = pltpu.VMEM((4, BLOCK, FFW), F32)
    hops = pltpu.VMEM((2, 4, ROWS, D), BF16)
    wide = pltpu.VMEM((ROWS, D), F32)
    dots = pltpu.VMEM((RING, 8, ROWS), F32)
    grad_input, gates_t, loss = pl.pallas_call(
        step_kernel,
        out_shape=[
            jax.ShapeDtypeStruct((ROWS, D), BF16),
            jax.ShapeDtypeStruct((8, ROWS), F32),
            jax.ShapeDtypeStruct((1, 1), F32),
        ],
        in_specs=[VMEM, VMEM, VMEM, ANY, ANY, ANY, VMEM, VMEM, VMEM, VMEM],
        out_specs=[VMEM, VMEM, SMEM],
        scratch_shapes=[
            pltpu.VMEM((D, FFW), BF16), pltpu.VMEM((D, FFW), BF16), pltpu.VMEM((FFW, D), BF16),
            pltpu.VMEM((RING, 16, ROWS), F32), pltpu.VMEM((16, ROWS), F32),
            selector, selector, selector, selector, selector, selector,
            pltpu.VMEM((4, 2 * ROWS, D), BF16), pairs, pairs, hidden, hidden, pres, pres,
            pairs, pairs, pairs, hops, hops,
            pltpu.VMEM((2, ROWS, ROWS), F32), wide, wide, pltpu.VMEM((ROWS, D), BF16),
            pltpu.VMEM((24, ROWS), F32), pltpu.VMEM((24, ROWS), F32),
            pltpu.VMEM((3, 8, 8, ROWS), F32), dots, dots,
            DMA((2, 4, 4)), DMA((2, 4, 4)), DMA((4,)), DMA((4,)), DMA((4, 4)), DMA((4, 4)),
            DMA((2, 4, 4)), DMA((2, 4, 4)), DMA((RING,)), DMA((RING,)), DMA((3,)),
            DMA((2,)), DMA((2,)), DMA((3, 8)), DMA((3,)), DMA((RING,)), DMA((RING,)),
        ],
        compiler_params=pltpu.CompilerParams(
            collective_id=0, has_side_effects=True, vmem_limit_bytes=64 * 1024 * 1024 - 65536
        ),
        name="step",
    )(frames_in, expert_ids, gate_values, gate_weight, up_weight, down_weight,
      norm_gain.reshape(1, D), pose_weight, target_pose, foot_contact)
    return (grad_input, gates_t[:TOP].T, loss[0, 0])


def solution(mesh):
    in_specs = (
        P(("seg", "ep"), None),
        P(("seg", "ep"), None),
        P(("seg", "ep"), None),
        P("ep", None, None),
        P("ep", None, None),
        P("ep", None, None),
        P(),
        P(),
        P(("seg", "ep"), None),
        P(("seg", "ep"), None),
    )
    out_specs = (P(("seg", "ep"), None), P(("seg", "ep"), None), P())
    return jax.shard_map(
        per_device, mesh=mesh, in_specs=in_specs, out_specs=out_specs, check_vma=False
    )
```

```python
import jax
import jax.numpy as jnp
from jax import lax
from jax.experimental import pallas as pl
from jax.experimental.pallas import tpu as pltpu
from jax.sharding import PartitionSpec as P

MESH = pl.DeviceIdType.MESH
epsilon = 1e-06
foot_weight = 2.0

RING = 8
GROUP = 8
ROWS = 128
CAP = 12
TOP = 6
D = 2048
POSE = 256
FEET = 4
FFW = 768
CHUNK = 512
PAIR = 2 * CAP
BLOCK = GROUP * PAIR
F32 = jnp.float32
BF16 = jnp.bfloat16

PLACE = {0: 0, 1: 1, 7: 2, 2: 3, 6: 4, 3: 5, 5: 6, 4: 7}


def cols(c):
    return pl.ds(c * CHUNK, CHUNK)


class Place:
    def __init__(self):
        ep = lax.axis_index("ep")
        self.z = lax.div(ep, GROUP)
        self.g = lax.rem(ep, GROUP)
        self.seg = lax.axis_index("seg")
        self.segs = lax.axis_size("seg")
        self.index = self.seg * (RING * GROUP) + ep

    def ring(self, distance):
        return {"ep": lax.rem(self.z + distance + RING, RING) * GROUP + self.g}

    def mate(self, offset):
        return lax.rem(self.g + offset, GROUP)

    def group(self, offset):
        return {"ep": self.z * GROUP + self.mate(offset)}

    def segment(self, offset):
        return {"seg": lax.rem(self.seg + offset, self.segs)}

    def next(self, offset):
        devices = RING * GROUP * self.segs
        index = lax.rem(self.index + offset + devices, devices)
        return {"seg": lax.div(index, RING * GROUP), "ep": lax.rem(index, RING * GROUP)}

    def barrier(self):
        semaphore = pltpu.get_barrier_semaphore()
        for o in (-1, 1):
            pl.semaphore_signal(semaphore, inc=1, device_id=self.ring(o), device_id_type=MESH)
        for o in range(1, GROUP):
            pl.semaphore_signal(semaphore, inc=1, device_id=self.group(o), device_id_type=MESH)
        for o in range(1, self.segs):
            pl.semaphore_signal(semaphore, inc=1, device_id=self.segment(o), device_id_type=MESH)
        for o in (-1, 1):
            pl.semaphore_signal(semaphore, inc=1, device_id=self.next(o), device_id_type=MESH)
        pl.semaphore_wait(semaphore, GROUP + self.segs + 2)


def remote(src, dst, send_sem, recv_sem, device):
    return pltpu.make_async_remote_copy(
        src_ref=src, dst_ref=dst, send_sem=send_sem, recv_sem=recv_sem,
        device_id=device, device_id_type=MESH,
    )


def slot_rows(ids_t):
    experts = lax.broadcasted_iota(jnp.int32, (RING * GROUP, ROWS), 0)
    chosen = jnp.zeros((RING * GROUP, ROWS), F32)
    for k in range(TOP):
        chosen = chosen + jnp.where(ids_t[k : k + 1, :] == experts, 1.0, 0.0)
    before = lax.broadcasted_iota(jnp.int32, (ROWS, ROWS), 0) < lax.broadcasted_iota(
        jnp.int32, (ROWS, ROWS), 1
    )
    earlier = jnp.dot(
        chosen.astype(BF16), jnp.where(before, 1.0, 0.0).astype(BF16), preferred_element_type=F32
    )
    table = []
    for k in range(TOP):
        ids = ids_t[k : k + 1, :]
        rank = jnp.sum(jnp.where(ids == experts, earlier, 0.0), axis=0, keepdims=True)
        table.append(jnp.where(rank < CAP, ids.astype(F32) * CAP + rank, -1.0))
    return jnp.concatenate(table, axis=0)


def row_slots(z, half):
    r = lax.broadcasted_iota(jnp.int32, (256, ROWS), 0)
    dest = jnp.zeros((256, ROWS), jnp.int32)
    for m in range(1, GROUP):
        dest = dest + jnp.where(r >= PAIR * m, 1, 0)
    within = r - PAIR * dest
    slot = within - CAP * half
    mine = (slot >= 0) & (slot < CAP) & (r < BLOCK)
    return jnp.where(mine, (z * GROUP + dest) * CAP + slot, -7).astype(F32)


def build_picks(z, tab, p, pick, pick_t, gate_hi, gate_lo, gate_hi_t, gate_lo_t):
    for half in range(2):
        slots = row_slots(z, half)
        ones = jnp.zeros((256, ROWS), F32)
        gates = jnp.zeros((256, ROWS), F32)
        for k in range(TOP):
            hit = tab[2 * p + half, k : k + 1, :] == slots
            ones = jnp.where(hit, 1.0, ones)
            gates = jnp.where(hit, tab[2 * p + half, 8 + k : 9 + k, :], gates)
        hi = gates.astype(BF16).astype(F32)
        lo = gates - hi
        lanes = slice(ROWS * half, ROWS * half + ROWS)
        pick[p, :, lanes] = ones.astype(BF16)
        gate_hi[p, :, lanes] = hi.astype(BF16)
        gate_lo[p, :, lanes] = lo.astype(BF16)
        pick_t[p, lanes, :] = ones.T.astype(BF16)
        gate_hi_t[p, lanes, :] = hi.T.astype(BF16)
        gate_lo_t[p, lanes, :] = lo.T.astype(BF16)


def dispatch(at, rows, zbuf, gbuf, xrecv, sems, tables, prepare, selectors, experts_of):
    zs, zr, xs, xr = sems

    def up_to(s):
        return (s, 0) if s < 4 else (3, ROWS)

    def plus(s, c):
        src = rows if s == 1 else zbuf.at[s - 1, pl.ds(0, ROWS)]
        p, r = up_to(s)
        return remote(src.at[:, cols(c)], zbuf.at[p, pl.ds(r, ROWS), cols(c)],
                      zs.at[0, s - 1, c], zr.at[0, s - 1, c], at.ring(1))

    def minus(s, c):
        src = rows if s == 1 else zbuf.at[s - 2, pl.ds(ROWS, ROWS)]
        return remote(src.at[:, cols(c)], zbuf.at[s - 1, pl.ds(ROWS, ROWS), cols(c)],
                      zs.at[1, s - 1, c], zr.at[1, s - 1, c], at.ring(-1))

    def has_plus(s, c):
        return s < 4 or (s == 4 and c < 2)

    def has_minus(s, c):
        return s < 4 or (s == 4 and c >= 2)

    def table_copies(s):
        if not tables:
            return []
        tab, ts, tr = tables
        j = (RING - s + 1) % RING
        copies = [remote(tab.at[PLACE[j]], tab.at[PLACE[RING - s]], ts.at[0, s - 1], tr.at[0, s - 1],
                         at.ring(1))]
        if s < 4:
            copies.append(remote(tab.at[PLACE[s - 1]], tab.at[PLACE[s]], ts.at[1, s - 1],
                                 tr.at[1, s - 1], at.ring(-1)))
        return copies

    for copy in table_copies(1):
        copy.start()
    for c in range(4):
        plus(1, c).start()
        minus(1, c).start()
    zbuf[0, 0:ROWS, :] = rows[...]
    for s in range(1, 5):
        p = s - 1
        for copy in table_copies(s):
            copy.wait_recv()
        if s < 4:
            for copy in table_copies(s + 1):
                copy.start()
        for i, c in enumerate((0, 1, 2, 3) if s < 4 else (0, 2, 1, 3)):
            if has_plus(s, c):
                plus(s, c).wait_recv()
            if has_minus(s, c):
                minus(s, c).wait_recv()
            if s < 4:
                if has_plus(s + 1, c):
                    plus(s + 1, c).start()
                if has_minus(s + 1, c):
                    minus(s + 1, c).start()
            if i == 0:
                prepare(p)
            block = zbuf[p, :, c * CHUNK : (c + 1) * CHUNK]
            picked = jnp.zeros((BLOCK, CHUNK), F32)
            for selector in selectors:
                picked = picked + jnp.dot(selector[p, 0:BLOCK, :], block, preferred_element_type=F32)
            gbuf[p, :, :, c * CHUNK : (c + 1) * CHUNK] = picked.astype(BF16).reshape(
                GROUP, PAIR, CHUNK
            )
            for o in range(1, GROUP):
                remote(gbuf.at[p, at.mate(o), :, cols(c)], xrecv.at[p, at.g, :, cols(c)],
                       xs.at[p], xr.at[p], at.group(o)).start()
        xrecv[p, at.g] = gbuf[p, at.g]
        if s >= 2:
            arrive(at, p - 1, gbuf, xrecv, xs, xr)
            experts_of(p - 1)
    arrive(at, 3, gbuf, xrecv, xs, xr)
    for s in range(1, 5):
        for copy in table_copies(s):
            copy.wait_send()
        for c in range(4):
            if has_plus(s, c):
                plus(s, c).wait_send()
            if has_minus(s, c):
                minus(s, c).wait_send()


def arrive(at, p, gbuf, xrecv, xs, xr):
    whole = remote(gbuf.at[p, pl.ds(0, GROUP - 1)], xrecv.at[p, pl.ds(0, GROUP - 1)],
                   xs.at[p], xr.at[p], at.group(1))
    whole.wait_send()
    whole.wait_recv()


BACK_ORDER = [(3, 0), (3, 2), (3, 1), (3, 3)] + [(p, c) for p in (2, 1, 0) for c in (2, 3, 0, 1)]
AHEAD = 6


def combine(at, ybuf, crecv, rsend, rrecv, sems, selectors_t, between, finish):
    cs, cr, rs, rr = sems
    seen = set()
    waiting = list(BACK_ORDER)

    def send_back():
        if waiting:
            p, c = waiting.pop(0)
            for o in range(1, GROUP):
                remote(ybuf.at[p, at.mate(o), :, cols(c)], crecv.at[p, at.g, :, cols(c)],
                       cs.at[p, c], cr.at[p, c], at.group(o)).start()
            window = slice(c * CHUNK, (c + 1) * CHUNK)
            crecv[p, at.g, :, window] = ybuf[p, at.g, :, window]

    for i in range(AHEAD):
        send_back()

    def partial(p, half, c):
        if (p, c) not in seen:
            seen.add((p, c))
            send_back()
            whole = remote(ybuf.at[p, pl.ds(0, GROUP - 1), :, cols(c)],
                           crecv.at[p, pl.ds(0, GROUP - 1), :, cols(c)],
                           cs.at[p, c], cr.at[p, c], at.group(1))
            whole.wait_send()
            whole.wait_recv()
        block = crecv[p, :, :, c * CHUNK : (c + 1) * CHUNK].reshape(BLOCK, CHUNK)
        total = jnp.zeros((ROWS, CHUNK), F32)
        for selector in selectors_t:
            total = total + jnp.dot(
                selector[p, half * ROWS : (half + 1) * ROWS, 0:BLOCK], block,
                preferred_element_type=F32,
            )
        return total

    def has(way, t, c):
        return t > 1 or (c < 2) == (way == 0)

    def hop(way, t, c):
        return remote(rsend.at[way, t - 1, :, cols(c)], rrecv.at[way, t - 1, :, cols(c)],
                      rs.at[way, t - 1, c], rr.at[way, t - 1, c], at.ring(1 if way == 0 else -1))

    def unit(way, t, c):
        if not has(way, t, c):
            return
        p, half = (4 - t, 1) if way == 0 or t == 1 else (5 - t, 0)
        total = partial(p, half, c)
        window = slice(c * CHUNK, (c + 1) * CHUNK)
        if t > 1 and has(way, t - 1, c):
            hop(way, t - 1, c).wait_recv()
            total = total + rrecv[way, t - 2, :, window].astype(F32)
        rsend[way, t - 1, :, window] = total.astype(BF16)
        hop(way, t, c).start()

    for t in range(1, 5):
        for c in range(4):
            c = c if t > 1 else (0, 2, 1, 3)[c]
            unit(0, t, c if t == 1 else c ^ 2)
            unit(1, t, c)
        between(t)
    for c in range(4):
        total = partial(0, 0, c)
        window = slice(c * CHUNK, (c + 1) * CHUNK)
        for way in range(2):
            hop(way, 4, c).wait_recv()
            total = total + rrecv[way, 3, :, window].astype(F32)
        finish(c, total)
    for t in range(1, 5):
        for c in range(4):
            for way in range(2):
                if has(way, t, c):
                    hop(way, t, c).wait_send()


def step_kernel(rows, ids, gates, wg_hbm, wu_hbm, wd_hbm, gain, pose_weight, target, contact,
                grad_in, gates_out, loss_out,
                wg, wu, wd, tab, pick, pick_t, gate_hi, gate_lo, gate_hi_t, gate_lo_t,
                zbuf, gbuf, xrecv, hidden, hidden2, gate_pre, up_pre, ybuf, crecv, crecv2, rsend, rrecv,
                turn, state, grad_state, moe_grad, foot, foot_recv, tiles, dots, dots_recv,
                zs, zr, xs, xr, cs, cr, rs, rr, ts, tr, ws, fs, fr, ls, lr, ds, dr):
    at = Place()
    loads = [pltpu.make_async_copy(a.at[0], b, ws.at[i])
             for i, (a, b) in enumerate(((wg_hbm, wg), (wu_hbm, wu), (wd_hbm, wd)))]
    for load in loads:
        load.start()
    tab_own = tab.at[0]
    tab_own[...] = jnp.zeros((16, ROWS), F32)
    tab_own[0:TOP, :] = slot_rows(ids[...])
    tab_own[8 : 8 + TOP, :] = gates[...]
    turn[...] = jnp.zeros((ROWS, ROWS), F32)
    turn[0:FEET, :] = contact[...].astype(F32)
    contact_columns = turn[...].T
    lanes = lax.broadcasted_iota(jnp.int32, (ROWS, ROWS), 1)
    contacts = jnp.zeros((ROWS, ROWS), F32)
    for k in range(FEET):
        here = (lanes >= 3 * k) & (lanes < 3 * k + 3)
        contacts = jnp.where(here, contact_columns[:, k : k + 1], contacts)
    turn[...] = contacts
    at.barrier()
    across = (((1,), (1,)), ((), ()))

    def picks(p):
        build_picks(at.z, tab, p, pick, pick_t, gate_hi, gate_lo, gate_hi_t, gate_lo_t)

    first = []

    def experts_forward(p):
        if not first:
            first.append(1)
            for load in loads:
                load.wait()

        def up_step(n, carry):
            window = pl.ds(pl.multiple_of(n * 256, 256), 256)
            x = xrecv[p].reshape(BLOCK, D)
            a = jnp.dot(x, wg[:, window], preferred_element_type=F32)
            b = jnp.dot(x, wu[:, window], preferred_element_type=F32)
            gate_pre[p, :, window] = a
            up_pre[p, :, window] = b
            hidden[:, window] = (a * jax.nn.sigmoid(a) * b).astype(BF16)
            return carry

        lax.fori_loop(0, FFW // 256, up_step, 0)

        def down_step(n, carry):
            window = pl.ds(pl.multiple_of(n * 256, 256), 256)
            y = jnp.dot(hidden[...], wd[:, window], preferred_element_type=F32)
            ybuf[p, :, :, window] = y.astype(BF16).reshape(GROUP, PAIR, 256)
            return carry

        lax.fori_loop(0, D // 256, down_step, 0)

    dispatch(at, rows, zbuf, gbuf, xrecv, (zs, zr, xs, xr), (tab, ts, tr), picks, (pick,),
             experts_forward)
    experts_forward(3)
    squares = []

    def finish_state(c, total):
        window = slice(c * CHUNK, (c + 1) * CHUNK)
        sums = rows[:, window].astype(F32) + total
        state[:, window] = sums
        squares.append(jnp.sum(sums * sums, axis=1, keepdims=True))

    combine(at, ybuf, crecv, rsend, rrecv, (cs, cr, rs, rr), (gate_hi_t, gate_lo_t),
            lambda t: None, finish_state)

    inverse = lax.rsqrt((squares[0] + squares[1] + squares[2] + squares[3]) / D + epsilon)
    pose = jnp.zeros((ROWS, POSE), F32)
    for c in range(4):
        window = slice(c * CHUNK, (c + 1) * CHUNK)
        normed = (state[:, window] * inverse * gain[:, window]).astype(BF16)
        pose = pose + jnp.dot(normed, pose_weight[window, :], preferred_element_type=F32)
    place = pl.multiple_of(at.index * ROWS, ROWS)
    frames = lax.broadcasted_iota(jnp.int32, (ROWS, 1), 0) + place
    frames_all = RING * GROUP * ROWS * at.segs
    horizon = 0.5 + frames.astype(F32) / (frames_all - 1)
    contacts = turn[...]
    feet = pose[:, 0:ROWS]
    foot[0:8, :] = feet[0:8]
    foot[8:16, :] = contacts[0:8]
    foot[16:24, :] = feet[ROWS - 8 :]
    to_next = remote(foot.at[pl.ds(16, 8)], foot_recv.at[pl.ds(16, 8)], fs.at[0], fr.at[0], at.next(1))
    to_last = remote(foot.at[pl.ds(0, 16)], foot_recv.at[pl.ds(0, 16)], fs.at[1], fr.at[1], at.next(-1))
    to_next.start()
    to_last.start()
    error = pose - target[...]
    grad_pose = horizon * error
    grad_far = grad_pose[:, ROWS:].astype(BF16)
    squared = grad_pose * error
    grad_parts = [
        lax.dot_general(grad_far, pose_weight[c * CHUNK : (c + 1) * CHUNK, ROWS:], across,
                        preferred_element_type=F32) for c in range(4)]
    for c in range(4):
        grad_state[:, c * CHUNK : (c + 1) * CHUNK] = grad_parts[c]
    to_next.wait_recv()
    to_last.wait_recv()
    row = lax.broadcasted_iota(jnp.int32, (ROWS, ROWS), 0)
    earlier = jnp.where(row == 0, foot_recv[23:24, :], pltpu.roll(feet, 1, 0))
    velocity = jnp.where(frames > 0, feet - earlier, 0.0)
    pull = foot_weight * horizon * contacts * velocity
    next_horizon = 0.5 + (place + ROWS).astype(F32) / (frames_all - 1)
    next_pull = foot_weight * next_horizon * foot_recv[8:9, :] * (foot_recv[0:1, :] - feet[ROWS - 1 :])
    next_pull = jnp.where(frames[ROWS - 1 :] < frames_all - 1, next_pull, 0.0)
    later = jnp.where(row == ROWS - 1, next_pull, pltpu.roll(pull, ROWS - 1, 0))
    terms = squared[:, 0:ROWS] + squared[:, ROWS:] + pull * velocity
    grad_near = (grad_pose[:, 0:ROWS] + (pull - later)).astype(BF16)
    products = jnp.zeros((ROWS, 1), F32)
    for c in range(4):
        window = slice(c * CHUNK, (c + 1) * CHUNK)
        grad_normed = grad_state[:, window] + lax.dot_general(
            grad_near, pose_weight[window, 0:ROWS], across, preferred_element_type=F32
        )
        scaled = grad_normed * gain[:, window]
        grad_state[:, window] = scaled
        products = products + jnp.sum(scaled * (state[:, window] * inverse), axis=1, keepdims=True)
    products = products / D
    for c in range(4):
        window = slice(c * CHUNK, (c + 1) * CHUNK)
        grads = inverse * (grad_state[:, window] - state[:, window] * inverse * products)
        grad_state[:, window] = grads
        moe_grad[:, window] = grads.astype(BF16)
    to_next.wait_send()
    to_last.wait_send()

    tile = jnp.zeros((8, ROWS), F32)
    for r in range(0, ROWS, 8):
        tile = tile + terms[r : r + 8]

    def share(stage, here, size, device, value):
        tiles[stage, here] = value
        sends = [remote(tiles.at[stage, here], tiles.at[stage, here], ls.at[stage, o], lr.at[stage],
                        device(o)) for o in range(1, size)]
        for send in sends:
            send.start()
        return sends

    def gather_tile(stage, size, sends):
        remote(tiles.at[stage, pl.ds(0, size - 1)], tiles.at[stage, pl.ds(0, size - 1)],
               ls.at[stage, 0], lr.at[stage], at.ring(1)).wait_recv()
        for send in sends:
            send.wait_send()
        total = tiles[stage, 0]
        for i in range(1, size):
            total = total + tiles[stage, i]
        return total

    shares = []

    def experts_backward(p):
        if p == 0:
            value = gather_tile(0, RING, shares.pop())
            shares.append(share(1, at.g, GROUP, at.group, value))
        if p == 1:
            value = gather_tile(1, GROUP, shares.pop())
            shares.append(share(2, at.seg, at.segs, at.segment, value))

        def down_step(n, carry):
            window = pl.ds(pl.multiple_of(n * 256, 256), 256)
            x = xrecv[p].reshape(BLOCK, D)
            grad = lax.dot_general(x, wd[window, :], across, preferred_element_type=F32)
            a = gate_pre[p, :, window]
            s = jax.nn.sigmoid(a)
            hidden[:, window] = (grad * up_pre[p, :, window] * (s * (1.0 + a * (1.0 - s)))).astype(BF16)
            hidden2[:, window] = (grad * (a * s)).astype(BF16)
            return carry

        lax.fori_loop(0, FFW // 256, down_step, 0)

        def up_step(n, carry):
            window = pl.ds(pl.multiple_of(n * 256, 256), 256)
            y = lax.dot_general(hidden[...], wg[window, :], across, preferred_element_type=F32)
            y = y + lax.dot_general(hidden2[...], wu[window, :], across, preferred_element_type=F32)
            ybuf[p, :, :, window] = y.astype(BF16).reshape(GROUP, PAIR, 256)
            return carry

        lax.fori_loop(0, D // 256, up_step, 0)
        if p < 3:
            gate_dots(p)

    def gate_dots(p):
        products = lax.dot_general(crecv[p].reshape(BLOCK, D), zbuf[p], across,
                                   preferred_element_type=F32)
        for half in range(2):
            slots = row_slots(at.z, half)[0:BLOCK]
            mine = products[:, ROWS * half : ROWS * half + ROWS]
            picked = [jnp.sum(jnp.where(tab[2 * p + half, k : k + 1, :] == slots, mine, 0.0),
                              axis=0, keepdims=True) for k in range(TOP)]
            dots[2 * p + half] = jnp.concatenate(picked + [jnp.zeros((2, ROWS), F32)], axis=0)

    def share_loss(p):
        if p == 0:
            shares.append(share(0, at.z, RING, at.ring, tile))

    dispatch(at, moe_grad, zbuf, gbuf, xrecv, (zs, zr, xs, xr), None, share_loss, (gate_hi, gate_lo),
             experts_backward)
    experts_backward(3)
    dot_sends = [remote(dots.at[PLACE[o]], dots_recv.at[PLACE[RING - o]], ds.at[o],
                        dr.at[PLACE[RING - o]], at.ring(o)) for o in range(1, RING)]

    def last_dots(t):
        if t == 1:
            gate_dots(3)
            for send in dot_sends:
                send.start()

    def finish_input(c, total):
        window = slice(c * CHUNK, (c + 1) * CHUNK)
        grad_in[:, window] = (grad_state[:, window] + total).astype(BF16)

    combine(at, ybuf, crecv2, rsend, rrecv, (cs, cr, rs, rr), (pick_t,), last_dots, finish_input)
    loss = gather_tile(2, at.segs, shares.pop())
    loss_out[0, 0] = jnp.sum(loss) * (0.5 / (frames_all * POSE))
    for send in dot_sends:
        send.wait_recv()
    total = dots[0]
    for o in range(1, RING):
        total = total + dots_recv[PLACE[RING - o]]
    gates_out[...] = total[0:TOP]
    for send in dot_sends:
        send.wait_send()


VMEM = pl.BlockSpec(memory_space=pltpu.VMEM)
SMEM = pl.BlockSpec(memory_space=pltpu.SMEM)
ANY = pl.BlockSpec(memory_space=pl.ANY)
DMA = pltpu.SemaphoreType.DMA


def per_device(
    frames_in,
    expert_ids,
    gate_values,
    gate_weight,
    up_weight,
    down_weight,
    norm_gain,
    pose_weight,
    target_pose,
    foot_contact,
):
    segs = lax.axis_size("seg")
    selector = pltpu.VMEM((4, 256, 256), BF16)
    pairs = pltpu.VMEM((4, GROUP, PAIR, D), BF16)
    hidden = pltpu.VMEM((BLOCK, FFW), BF16)
    pres = pltpu.VMEM((4, BLOCK, FFW), F32)
    hops = pltpu.VMEM((2, 4, ROWS, D), BF16)
    wide = pltpu.VMEM((ROWS, D), F32)
    dots = pltpu.VMEM((RING, 8, ROWS), F32)
    grad_input, gates_t, loss = pl.pallas_call(
        step_kernel,
        out_shape=[
            jax.ShapeDtypeStruct((ROWS, D), BF16),
            jax.ShapeDtypeStruct((TOP, ROWS), F32),
            jax.ShapeDtypeStruct((1, 1), F32),
        ],
        in_specs=[VMEM, VMEM, VMEM, ANY, ANY, ANY, VMEM, VMEM, VMEM, VMEM],
        out_specs=[VMEM, VMEM, SMEM],
        scratch_shapes=[
            pltpu.VMEM((D, FFW), BF16), pltpu.VMEM((D, FFW), BF16), pltpu.VMEM((FFW, D), BF16),
            pltpu.VMEM((RING, 16, ROWS), F32),
            selector, selector, selector, selector, selector, selector,
            pltpu.VMEM((4, 2 * ROWS, D), BF16), pairs, pairs, hidden, hidden, pres, pres,
            pairs, pairs, pairs, hops, hops,
            pltpu.VMEM((ROWS, ROWS), F32), wide, wide, pltpu.VMEM((ROWS, D), BF16),
            pltpu.VMEM((24, ROWS), F32), pltpu.VMEM((24, ROWS), F32),
            pltpu.VMEM((3, 8, 8, ROWS), F32), dots, dots,
            DMA((2, 4, 4)), DMA((2, 4, 4)), DMA((4,)), DMA((4,)), DMA((4, 4)), DMA((4, 4)),
            DMA((2, 4, 4)), DMA((2, 4, 4)), DMA((2, 4)), DMA((2, 4)), DMA((3,)),
            DMA((2,)), DMA((2,)), DMA((3, 8)), DMA((3,)), DMA((RING,)), DMA((RING,)),
        ],
        compiler_params=pltpu.CompilerParams(
            collective_id=0, has_side_effects=True, vmem_limit_bytes=64 * 1024 * 1024 - 65536
        ),
        name="step",
    )(frames_in, expert_ids.T, gate_values.T, gate_weight, up_weight, down_weight,
      norm_gain.reshape(1, D), pose_weight, target_pose, foot_contact.T)
    return (grad_input, gates_t.T, loss[0, 0])


def solution(mesh):
    in_specs = (
        P(("seg", "ep"), None),
        P(("seg", "ep"), None),
        P(("seg", "ep"), None),
        P("ep", None, None),
        P("ep", None, None),
        P("ep", None, None),
        P(),
        P(),
        P(("seg", "ep"), None),
        P(("seg", "ep"), None),
    )
    out_specs = (P(("seg", "ep"), None), P(("seg", "ep"), None), P())
    return jax.shard_map(
        per_device, mesh=mesh, in_specs=in_specs, out_specs=out_specs, check_vma=False
    )
```

```python
import jax
import jax.numpy as jnp
from jax import lax
from jax.experimental import pallas as pl
from jax.experimental.pallas import tpu as pltpu
from jax.sharding import PartitionSpec as P

MESH = pl.DeviceIdType.MESH
epsilon = 1e-06
foot_weight = 2.0

RING = 8
GROUP = 8
ROWS = 128
CAP = 12
TOP = 6
D = 2048
POSE = 256
FEET = 4
FFW = 768
CHUNK = 512
PAIR = 2 * CAP
BLOCK = GROUP * PAIR
F32 = jnp.float32
BF16 = jnp.bfloat16

PLACE = {0: 0, 1: 1, 7: 2, 2: 3, 6: 4, 3: 5, 5: 6, 4: 7}


def cols(c):
    return pl.ds(c * CHUNK, CHUNK)


class Place:
    def __init__(self):
        ep = lax.axis_index("ep")
        self.z = lax.div(ep, GROUP)
        self.g = lax.rem(ep, GROUP)
        self.seg = lax.axis_index("seg")
        self.segs = lax.axis_size("seg")
        self.index = self.seg * (RING * GROUP) + ep

    def ring(self, distance):
        return {"ep": lax.rem(self.z + distance + RING, RING) * GROUP + self.g}

    def mate(self, offset):
        return lax.rem(self.g + offset, GROUP)

    def group(self, offset):
        return {"ep": self.z * GROUP + self.mate(offset)}

    def segment(self, offset):
        return {"seg": lax.rem(self.seg + offset, self.segs)}

    def next(self, offset):
        devices = RING * GROUP * self.segs
        index = lax.rem(self.index + offset + devices, devices)
        return {"seg": lax.div(index, RING * GROUP), "ep": lax.rem(index, RING * GROUP)}

    def greet(self):
        semaphore = pltpu.get_barrier_semaphore()
        for o in (-1, 1):
            pl.semaphore_signal(semaphore, inc=1, device_id=self.ring(o), device_id_type=MESH)
        for o in range(1, GROUP):
            pl.semaphore_signal(semaphore, inc=1, device_id=self.group(o), device_id_type=MESH)
        for o in range(1, self.segs):
            pl.semaphore_signal(semaphore, inc=1, device_id=self.segment(o), device_id_type=MESH)
        for o in (-1, 1):
            pl.semaphore_signal(semaphore, inc=1, device_id=self.next(o), device_id_type=MESH)

    def meet(self):
        pl.semaphore_wait(pltpu.get_barrier_semaphore(), GROUP + self.segs + 2)


def remote(src, dst, send_sem, recv_sem, device):
    return pltpu.make_async_remote_copy(
        src_ref=src, dst_ref=dst, send_sem=send_sem, recv_sem=recv_sem,
        device_id=device, device_id_type=MESH,
    )


def slot_rows(ids_t):
    experts = lax.broadcasted_iota(jnp.int32, (RING * GROUP, ROWS), 0)
    chosen = jnp.zeros((RING * GROUP, ROWS), F32)
    for k in range(TOP):
        chosen = chosen + jnp.where(ids_t[k : k + 1, :] == experts, 1.0, 0.0)
    before = lax.broadcasted_iota(jnp.int32, (ROWS, ROWS), 0) < lax.broadcasted_iota(
        jnp.int32, (ROWS, ROWS), 1
    )
    earlier = jnp.dot(
        chosen.astype(BF16), jnp.where(before, 1.0, 0.0).astype(BF16), preferred_element_type=F32
    )
    table = []
    for k in range(TOP):
        ids = ids_t[k : k + 1, :]
        rank = jnp.sum(jnp.where(ids == experts, earlier, 0.0), axis=0, keepdims=True)
        table.append(jnp.where(rank < CAP, ids.astype(F32) * CAP + rank, -1.0))
    return jnp.concatenate(table, axis=0)


def row_slots(z, half):
    r = lax.broadcasted_iota(jnp.int32, (256, ROWS), 0)
    dest = jnp.zeros((256, ROWS), jnp.int32)
    for m in range(1, GROUP):
        dest = dest + jnp.where(r >= PAIR * m, 1, 0)
    within = r - PAIR * dest
    slot = within - CAP * half
    mine = (slot >= 0) & (slot < CAP) & (r < BLOCK)
    return jnp.where(mine, (z * GROUP + dest) * CAP + slot, -7).astype(F32)


def build_picks(z, tab, p, pick, pick_t, gate_hi, gate_lo, gate_hi_t, gate_lo_t):
    for half in range(2):
        slots = row_slots(z, half)
        ones = jnp.zeros((256, ROWS), F32)
        gates = jnp.zeros((256, ROWS), F32)
        for k in range(TOP):
            hit = tab[2 * p + half, k : k + 1, :] == slots
            ones = jnp.where(hit, 1.0, ones)
            gates = jnp.where(hit, tab[2 * p + half, 8 + k : 9 + k, :], gates)
        hi = gates.astype(BF16).astype(F32)
        lo = gates - hi
        lanes = slice(ROWS * half, ROWS * half + ROWS)
        pick[p, :, lanes] = ones.astype(BF16)
        gate_hi[p, :, lanes] = hi.astype(BF16)
        gate_lo[p, :, lanes] = lo.astype(BF16)
        pick_t[p, lanes, :] = ones.T.astype(BF16)
        gate_hi_t[p, lanes, :] = hi.T.astype(BF16)
        gate_lo_t[p, lanes, :] = lo.T.astype(BF16)


def dispatch(at, rows, zbuf, gbuf, xrecv, sems, tables, prepare, selectors, experts_of):
    zs, zr, xs, xr = sems

    def up_to(s):
        return (s, 0) if s < 4 else (3, ROWS)

    def plus(s, c):
        src = rows if s == 1 else zbuf.at[s - 1, pl.ds(0, ROWS)]
        p, r = up_to(s)
        return remote(src.at[:, cols(c)], zbuf.at[p, pl.ds(r, ROWS), cols(c)],
                      zs.at[0, s - 1, c], zr.at[0, s - 1, c], at.ring(1))

    def minus(s, c):
        src = rows if s == 1 else zbuf.at[s - 2, pl.ds(ROWS, ROWS)]
        return remote(src.at[:, cols(c)], zbuf.at[s - 1, pl.ds(ROWS, ROWS), cols(c)],
                      zs.at[1, s - 1, c], zr.at[1, s - 1, c], at.ring(-1))

    def has_plus(s, c):
        return s < 4 or (s == 4 and c < 2)

    def has_minus(s, c):
        return s < 4 or (s == 4 and c >= 2)

    def table_copies(s):
        if not tables:
            return []
        tab, ts, tr = tables
        j = (RING - s + 1) % RING
        copies = [remote(tab.at[PLACE[j]], tab.at[PLACE[RING - s]], ts.at[0, s - 1], tr.at[0, s - 1],
                         at.ring(1))]
        if s < 4:
            copies.append(remote(tab.at[PLACE[s - 1]], tab.at[PLACE[s]], ts.at[1, s - 1],
                                 tr.at[1, s - 1], at.ring(-1)))
        return copies

    for copy in table_copies(1):
        copy.start()
    for c in range(4):
        plus(1, c).start()
        minus(1, c).start()
    for s in range(1, 5):
        p = s - 1
        for copy in table_copies(s):
            copy.wait_recv()
        if s < 4:
            for copy in table_copies(s + 1):
                copy.start()
        for i, c in enumerate((0, 1, 2, 3) if s < 4 else (0, 2, 1, 3)):
            if has_plus(s, c):
                plus(s, c).wait_recv()
            if has_minus(s, c):
                minus(s, c).wait_recv()
            if s < 4:
                if has_plus(s + 1, c):
                    plus(s + 1, c).start()
                if has_minus(s + 1, c):
                    minus(s + 1, c).start()
            if i == 0:
                prepare(p)
            block = zbuf[p, :, c * CHUNK : (c + 1) * CHUNK]
            picked = jnp.zeros((BLOCK, CHUNK), F32)
            for selector in selectors:
                picked = picked + jnp.dot(selector[p, 0:BLOCK, :], block, preferred_element_type=F32)
            gbuf[p, :, :, c * CHUNK : (c + 1) * CHUNK] = picked.astype(BF16).reshape(
                GROUP, PAIR, CHUNK
            )
            for o in range(1, GROUP):
                remote(gbuf.at[p, at.mate(o), :, cols(c)], xrecv.at[p, at.g, :, cols(c)],
                       xs.at[p], xr.at[p, c], at.group(o)).start()
        xrecv[p, at.g] = gbuf[p, at.g]
        if s >= 2:
            for c in range(4):
                arrive(at, p - 1, c, gbuf, xrecv, xs, xr)
            experts_of(p - 1)

    def drain():
        for p in range(4):
            remote(gbuf.at[p, pl.ds(0, GROUP - 1)], xrecv.at[p, pl.ds(0, GROUP - 1)],
                   xs.at[p], xr.at[p, 0], at.group(1)).wait_send()
        for s in range(1, 5):
            for copy in table_copies(s):
                copy.wait_send()
            for c in range(4):
                if has_plus(s, c):
                    plus(s, c).wait_send()
                if has_minus(s, c):
                    minus(s, c).wait_send()

    return drain


def arrive(at, p, c, gbuf, xrecv, xs, xr):
    remote(gbuf.at[p, pl.ds(0, GROUP - 1), :, cols(c)], xrecv.at[p, pl.ds(0, GROUP - 1), :, cols(c)],
           xs.at[p], xr.at[p, c], at.group(1)).wait_recv()


BACK_ORDER = [(3, 0), (3, 2), (3, 1), (3, 3)] + [(p, c) for p in (2, 1, 0) for c in (2, 3, 0, 1)]
AHEAD = 6
LAST_ORDER = (0, 2, 1, 3)


def combine(at, ybuf, crecv, rsend, rrecv, sems, selectors_t, produce, between, finish):
    cs, cr, rs, rr = sems
    seen = set()
    waiting = list(BACK_ORDER)

    def send_back():
        if waiting:
            p, c = waiting.pop(0)
            if p == 3:
                produce(c)
            for o in range(1, GROUP):
                remote(ybuf.at[p, at.mate(o), :, cols(c)], crecv.at[p, at.g, :, cols(c)],
                       cs.at[p, c], cr.at[p, c], at.group(o)).start()
            window = slice(c * CHUNK, (c + 1) * CHUNK)
            crecv[p, at.g, :, window] = ybuf[p, at.g, :, window]

    for i in range(AHEAD):
        send_back()

    def whole(p, c):
        return remote(ybuf.at[p, pl.ds(0, GROUP - 1), :, cols(c)],
                      crecv.at[p, pl.ds(0, GROUP - 1), :, cols(c)],
                      cs.at[p, c], cr.at[p, c], at.group(1))

    def partial(p, half, c):
        if (p, c) not in seen:
            seen.add((p, c))
            send_back()
            whole(p, c).wait_recv()
        block = crecv[p, :, :, c * CHUNK : (c + 1) * CHUNK].reshape(BLOCK, CHUNK)
        total = jnp.zeros((ROWS, CHUNK), F32)
        for selector in selectors_t:
            total = total + jnp.dot(
                selector[p, half * ROWS : (half + 1) * ROWS, 0:BLOCK], block,
                preferred_element_type=F32,
            )
        return total

    def has(way, t, c):
        return t > 1 or (c < 2) == (way == 0)

    def hop(way, t, c):
        return remote(rsend.at[way, t - 1, :, cols(c)], rrecv.at[way, t - 1, :, cols(c)],
                      rs.at[way, t - 1, c], rr.at[way, t - 1, c], at.ring(1 if way == 0 else -1))

    def unit(way, t, c):
        if not has(way, t, c):
            return
        p, half = (4 - t, 1) if way == 0 or t == 1 else (5 - t, 0)
        total = partial(p, half, c)
        window = slice(c * CHUNK, (c + 1) * CHUNK)
        if t > 1 and has(way, t - 1, c):
            hop(way, t - 1, c).wait_recv()
            total = total + rrecv[way, t - 2, :, window].astype(F32)
        rsend[way, t - 1, :, window] = total.astype(BF16)
        hop(way, t, c).start()

    for t in range(1, 5):
        for c in range(4):
            c = c if t > 1 else (0, 2, 1, 3)[c]
            unit(0, t, c if t == 1 else c ^ 2)
            unit(1, t, c)
        between(t)
    for c in range(4):
        total = partial(0, 0, c)
        window = slice(c * CHUNK, (c + 1) * CHUNK)
        for way in range(2):
            hop(way, 4, c).wait_recv()
            total = total + rrecv[way, 3, :, window].astype(F32)
        finish(c, total)
    for t in range(1, 5):
        for c in range(4):
            whole(t - 1, c).wait_send()
            for way in range(2):
                if has(way, t, c):
                    hop(way, t, c).wait_send()


def step_kernel(rows_hbm, ids, gates, wg_hbm, wu_hbm, wd_hbm, gain, pose_hbm, target_hbm, contact,
                grad_hbm, gates_out, loss_out,
                wg, wu, wd, pose_weight, target, tab, pick, pick_t, gate_hi, gate_lo, gate_hi_t, gate_lo_t,
                zbuf, gbuf, xrecv, hidden, hidden2, grad_hidden, gate_pre, up_pre, ybuf, crecv, crecv2, rsend, rrecv,
                turn, state, grad_state, grad_in, foot, foot_recv, tiles, dots, dots_recv,
                zs, zr, xs, xr, cs, cr, rs, rr, ts, tr, ws, fs, fr, ls, lr, ds, dr):
    at = Place()
    loads = [pltpu.make_async_copy(a.at[0], b, ws.at[i])
             for i, (a, b) in enumerate(((wg_hbm, wg), (wu_hbm, wu), (wd_hbm, wd)))]
    loads += [pltpu.make_async_copy(pose_hbm, pose_weight, ws.at[3]),
              pltpu.make_async_copy(target_hbm, target, ws.at[4])]
    own = zbuf.at[0, pl.ds(0, ROWS)]
    rows_load = pltpu.make_async_copy(rows_hbm, own, ws.at[5])
    rows_load.start()
    at.greet()
    for load in loads:
        load.start()
    tab_own = tab.at[0]
    tab_own[...] = jnp.zeros((16, ROWS), F32)
    tab_own[0:TOP, :] = slot_rows(ids[...])
    tab_own[8 : 8 + TOP, :] = gates[...]
    turn[...] = jnp.zeros((ROWS, ROWS), F32)
    turn[0:FEET, :] = contact[...].astype(F32)
    contact_columns = turn[...].T
    lanes = lax.broadcasted_iota(jnp.int32, (ROWS, ROWS), 1)
    contacts = jnp.zeros((ROWS, ROWS), F32)
    for k in range(FEET):
        here = (lanes >= 3 * k) & (lanes < 3 * k + 3)
        contacts = jnp.where(here, contact_columns[:, k : k + 1], contacts)
    turn[...] = contacts
    at.meet()
    rows_load.wait()
    across = (((1,), (1,)), ((), ()))

    def picks(p):
        build_picks(at.z, tab, p, pick, pick_t, gate_hi, gate_lo, gate_hi_t, gate_lo_t)

    first = []

    def experts_forward(p):
        if not first:
            first.append(1)
            for load in loads:
                load.wait()

        def up_step(n, carry):
            window = pl.ds(pl.multiple_of(n * 256, 256), 256)
            x = xrecv[p].reshape(BLOCK, D)
            a = jnp.dot(x, wg[:, window], preferred_element_type=F32)
            b = jnp.dot(x, wu[:, window], preferred_element_type=F32)
            gate_pre[p, :, window] = a
            up_pre[p, :, window] = b
            hidden[:, window] = (a * jax.nn.sigmoid(a) * b).astype(BF16)
            return carry

        lax.fori_loop(0, FFW // 256, up_step, 0)

        def down_step(n, carry):
            window = pl.ds(pl.multiple_of(n * 256, 256), 256)
            y = jnp.dot(hidden[...], wd[:, window], preferred_element_type=F32)
            ybuf[p, :, :, window] = y.astype(BF16).reshape(GROUP, PAIR, 256)
            return carry

        lax.fori_loop(0, D // 256, down_step, 0)

    drain = dispatch(at, own, zbuf, gbuf, xrecv, (zs, zr, xs, xr), (tab, ts, tr), picks, (pick,),
                     experts_forward)
    for i, c in enumerate(LAST_ORDER):
        arrive(at, 3, c, gbuf, xrecv, xs, xr)

        def up_part(n, carry):
            window = pl.ds(pl.multiple_of(n * 256, 256), 256)
            x = xrecv[3, :, :, c * CHUNK : (c + 1) * CHUNK].reshape(BLOCK, CHUNK)
            a = jnp.dot(x, wg[c * CHUNK : (c + 1) * CHUNK, window], preferred_element_type=F32)
            b = jnp.dot(x, wu[c * CHUNK : (c + 1) * CHUNK, window], preferred_element_type=F32)
            if i > 0:
                a = a + gate_pre[3, :, window]
                b = b + up_pre[3, :, window]
            gate_pre[3, :, window] = a
            up_pre[3, :, window] = b
            if i == 3:
                hidden[:, window] = (a * jax.nn.sigmoid(a) * b).astype(BF16)
            return carry

        lax.fori_loop(0, FFW // 256, up_part, 0)

    def last_forward(c):
        y = jnp.dot(hidden[...], wd[:, c * CHUNK : (c + 1) * CHUNK], preferred_element_type=F32)
        ybuf[3, :, :, c * CHUNK : (c + 1) * CHUNK] = y.astype(BF16).reshape(GROUP, PAIR, CHUNK)

    squares = []

    def finish_state(c, total):
        window = slice(c * CHUNK, (c + 1) * CHUNK)
        sums = zbuf[0, 0:ROWS, window].astype(F32) + total
        state[:, window] = sums
        squares.append(jnp.sum(sums * sums, axis=1, keepdims=True))

    combine(at, ybuf, crecv, rsend, rrecv, (cs, cr, rs, rr), (gate_hi_t, gate_lo_t),
            last_forward, lambda t: drain() if t == 1 else None, finish_state)

    inverse = lax.rsqrt((squares[0] + squares[1] + squares[2] + squares[3]) / D + epsilon)
    pose = jnp.zeros((ROWS, POSE), F32)
    for c in range(4):
        window = slice(c * CHUNK, (c + 1) * CHUNK)
        normed = (state[:, window] * inverse * gain[:, window]).astype(BF16)
        pose = pose + jnp.dot(normed, pose_weight[window, :], preferred_element_type=F32)
    place = pl.multiple_of(at.index * ROWS, ROWS)
    frames = lax.broadcasted_iota(jnp.int32, (ROWS, 1), 0) + place
    frames_all = RING * GROUP * ROWS * at.segs
    horizon = 0.5 + frames.astype(F32) / (frames_all - 1)
    contacts = turn[...]
    feet = pose[:, 0:ROWS]
    foot[0:8, :] = feet[0:8]
    foot[8:16, :] = contacts[0:8]
    foot[16:24, :] = feet[ROWS - 8 :]
    to_next = remote(foot.at[pl.ds(16, 8)], foot_recv.at[pl.ds(16, 8)], fs.at[0], fr.at[0], at.next(1))
    to_last = remote(foot.at[pl.ds(0, 16)], foot_recv.at[pl.ds(0, 16)], fs.at[1], fr.at[1], at.next(-1))
    to_next.start()
    to_last.start()
    error = pose - target[...]
    grad_pose = horizon * error
    grad_far = grad_pose[:, ROWS:].astype(BF16)
    squared = grad_pose * error
    grad_parts = [
        lax.dot_general(grad_far, pose_weight[c * CHUNK : (c + 1) * CHUNK, ROWS:], across,
                        preferred_element_type=F32) for c in range(4)]
    for c in range(4):
        grad_state[:, c * CHUNK : (c + 1) * CHUNK] = grad_parts[c]
    to_next.wait_recv()
    to_last.wait_recv()
    row = lax.broadcasted_iota(jnp.int32, (ROWS, ROWS), 0)
    earlier = jnp.where(row == 0, foot_recv[23:24, :], pltpu.roll(feet, 1, 0))
    velocity = jnp.where(frames > 0, feet - earlier, 0.0)
    pull = foot_weight * horizon * contacts * velocity
    next_horizon = 0.5 + (place + ROWS).astype(F32) / (frames_all - 1)
    next_pull = foot_weight * next_horizon * foot_recv[8:9, :] * (foot_recv[0:1, :] - feet[ROWS - 1 :])
    next_pull = jnp.where(frames[ROWS - 1 :] < frames_all - 1, next_pull, 0.0)
    later = jnp.where(row == ROWS - 1, next_pull, pltpu.roll(pull, ROWS - 1, 0))
    terms = squared[:, 0:ROWS] + squared[:, ROWS:] + pull * velocity
    grad_near = (grad_pose[:, 0:ROWS] + (pull - later)).astype(BF16)
    products = jnp.zeros((ROWS, 1), F32)
    for c in range(4):
        window = slice(c * CHUNK, (c + 1) * CHUNK)
        grad_normed = grad_state[:, window] + lax.dot_general(
            grad_near, pose_weight[window, 0:ROWS], across, preferred_element_type=F32
        )
        scaled = grad_normed * gain[:, window]
        grad_state[:, window] = scaled
        products = products + jnp.sum(scaled * (state[:, window] * inverse), axis=1, keepdims=True)
    products = products / D
    for c in range(4):
        window = slice(c * CHUNK, (c + 1) * CHUNK)
        grads = inverse * (grad_state[:, window] - state[:, window] * inverse * products)
        grad_state[:, window] = grads
        zbuf[0, 0:ROWS, window] = grads.astype(BF16)
    to_next.wait_send()
    to_last.wait_send()

    tile = jnp.zeros((8, ROWS), F32)
    for r in range(0, ROWS, 8):
        tile = tile + terms[r : r + 8]

    def share(stage, here, size, device, value):
        tiles[stage, here] = value
        sends = [remote(tiles.at[stage, here], tiles.at[stage, here], ls.at[stage, o], lr.at[stage],
                        device(o)) for o in range(1, size)]
        for send in sends:
            send.start()
        return sends

    def gather_tile(stage, size, sends):
        remote(tiles.at[stage, pl.ds(0, size - 1)], tiles.at[stage, pl.ds(0, size - 1)],
               ls.at[stage, 0], lr.at[stage], at.ring(1)).wait_recv()
        for send in sends:
            send.wait_send()
        total = tiles[stage, 0]
        for i in range(1, size):
            total = total + tiles[stage, i]
        return total

    shares = []

    def experts_backward(p):
        if p == 0:
            value = gather_tile(0, RING, shares.pop())
            shares.append(share(1, at.g, GROUP, at.group, value))
        if p == 1:
            value = gather_tile(1, GROUP, shares.pop())
            shares.append(share(2, at.seg, at.segs, at.segment, value))

        def down_step(n, carry):
            window = pl.ds(pl.multiple_of(n * 256, 256), 256)
            x = xrecv[p].reshape(BLOCK, D)
            grad = lax.dot_general(x, wd[window, :], across, preferred_element_type=F32)
            a = gate_pre[p, :, window]
            s = jax.nn.sigmoid(a)
            hidden[:, window] = (grad * up_pre[p, :, window] * (s * (1.0 + a * (1.0 - s)))).astype(BF16)
            hidden2[:, window] = (grad * (a * s)).astype(BF16)
            return carry

        lax.fori_loop(0, FFW // 256, down_step, 0)

        def up_step(n, carry):
            window = pl.ds(pl.multiple_of(n * 256, 256), 256)
            y = lax.dot_general(hidden[...], wg[window, :], across, preferred_element_type=F32)
            y = y + lax.dot_general(hidden2[...], wu[window, :], across, preferred_element_type=F32)
            ybuf[p, :, :, window] = y.astype(BF16).reshape(GROUP, PAIR, 256)
            return carry

        lax.fori_loop(0, D // 256, up_step, 0)
        if p < 2:
            gate_dots(p)

    def gate_dots(p):
        products = lax.dot_general(crecv[p].reshape(BLOCK, D), zbuf[p], across,
                                   preferred_element_type=F32)
        for half in range(2):
            slots = row_slots(at.z, half)[0:BLOCK]
            mine = products[:, ROWS * half : ROWS * half + ROWS]
            picked = [jnp.sum(jnp.where(tab[2 * p + half, k : k + 1, :] == slots, mine, 0.0),
                              axis=0, keepdims=True) for k in range(TOP)]
            dots[2 * p + half] = jnp.concatenate(picked + [jnp.zeros((2, ROWS), F32)], axis=0)

    def share_loss(p):
        if p == 0:
            shares.append(share(0, at.z, RING, at.ring, tile))

    drain = dispatch(at, own, zbuf, gbuf, xrecv, (zs, zr, xs, xr), None, share_loss,
                     (gate_hi, gate_lo), experts_backward)
    for i, c in enumerate(LAST_ORDER):
        arrive(at, 3, c, gbuf, xrecv, xs, xr)

        def down_part(n, carry):
            window = pl.ds(pl.multiple_of(n * 256, 256), 256)
            x = xrecv[3, :, :, c * CHUNK : (c + 1) * CHUNK].reshape(BLOCK, CHUNK)
            grad = lax.dot_general(x, wd[window, c * CHUNK : (c + 1) * CHUNK], across,
                                   preferred_element_type=F32)
            if i > 0:
                grad = grad + grad_hidden[:, window]
            if i < 3:
                grad_hidden[:, window] = grad
            else:
                a = gate_pre[3, :, window]
                s = jax.nn.sigmoid(a)
                hidden[:, window] = (grad * up_pre[3, :, window] * (s * (1.0 + a * (1.0 - s)))).astype(BF16)
                hidden2[:, window] = (grad * (a * s)).astype(BF16)
            return carry

        lax.fori_loop(0, FFW // 256, down_part, 0)

    def last_backward(c):
        y = lax.dot_general(hidden[...], wg[c * CHUNK : (c + 1) * CHUNK, :], across,
                            preferred_element_type=F32)
        y = y + lax.dot_general(hidden2[...], wu[c * CHUNK : (c + 1) * CHUNK, :], across,
                                preferred_element_type=F32)
        ybuf[3, :, :, c * CHUNK : (c + 1) * CHUNK] = y.astype(BF16).reshape(GROUP, PAIR, CHUNK)

    dot_sends = [remote(dots.at[PLACE[o]], dots_recv.at[PLACE[RING - o]], ds.at[o],
                        dr.at[PLACE[RING - o]], at.ring(o)) for o in range(1, RING)]

    def last_dots(t):
        if t == 2:
            drain()
        if t == 1:
            gate_dots(2)
            gate_dots(3)
            for send in dot_sends:
                send.start()

    def finish_input(c, total):
        window = slice(c * CHUNK, (c + 1) * CHUNK)
        grad_in[:, window] = (grad_state[:, window] + total).astype(BF16)
        store(c).start()

    def store(c):
        return pltpu.make_async_copy(grad_in.at[:, cols(c)], grad_hbm.at[:, cols(c)], ws.at[c])

    combine(at, ybuf, crecv2, rsend, rrecv, (cs, cr, rs, rr), (pick_t,), last_backward,
            last_dots, finish_input)
    loss = gather_tile(2, at.segs, shares.pop())
    loss_out[0, 0] = jnp.sum(loss) * (0.5 / (frames_all * POSE))
    for send in dot_sends:
        send.wait_recv()
    total = dots[0]
    for o in range(1, RING):
        total = total + dots_recv[PLACE[RING - o]]
    gates_out[...] = total[0:TOP]
    for c in range(4):
        store(c).wait()
    for send in dot_sends:
        send.wait_send()


VMEM = pl.BlockSpec(memory_space=pltpu.VMEM)
SMEM = pl.BlockSpec(memory_space=pltpu.SMEM)
ANY = pl.BlockSpec(memory_space=pl.ANY)
DMA = pltpu.SemaphoreType.DMA


def per_device(
    frames_in,
    expert_ids,
    gate_values,
    gate_weight,
    up_weight,
    down_weight,
    norm_gain,
    pose_weight,
    target_pose,
    foot_contact,
):
    segs = lax.axis_size("seg")
    selector = pltpu.VMEM((4, 256, 256), BF16)
    pairs = pltpu.VMEM((4, GROUP, PAIR, D), BF16)
    hidden = pltpu.VMEM((BLOCK, FFW), BF16)
    pres = pltpu.VMEM((4, BLOCK, FFW), F32)
    hops = pltpu.VMEM((2, 4, ROWS, D), BF16)
    wide = pltpu.VMEM((ROWS, D), F32)
    dots = pltpu.VMEM((RING, 8, ROWS), F32)
    grad_input, gates_t, loss = pl.pallas_call(
        step_kernel,
        out_shape=[
            jax.ShapeDtypeStruct((ROWS, D), BF16),
            jax.ShapeDtypeStruct((TOP, ROWS), F32),
            jax.ShapeDtypeStruct((1, 1), F32),
        ],
        in_specs=[ANY, VMEM, VMEM, ANY, ANY, ANY, VMEM, ANY, ANY, VMEM],
        out_specs=[ANY, VMEM, SMEM],
        scratch_shapes=[
            pltpu.VMEM((D, FFW), BF16), pltpu.VMEM((D, FFW), BF16), pltpu.VMEM((FFW, D), BF16),
            pltpu.VMEM((D, POSE), BF16), pltpu.VMEM((ROWS, POSE), F32),
            pltpu.VMEM((RING, 16, ROWS), F32),
            selector, selector, selector, selector, selector, selector,
            pltpu.VMEM((4, 2 * ROWS, D), BF16), pairs, pairs, hidden, hidden, pltpu.VMEM((BLOCK, FFW), F32), pres, pres,
            pairs, pairs, pairs, hops, hops,
            pltpu.VMEM((ROWS, ROWS), F32), wide, wide, pltpu.VMEM((ROWS, D), BF16),
            pltpu.VMEM((24, ROWS), F32), pltpu.VMEM((24, ROWS), F32),
            pltpu.VMEM((3, 8, 8, ROWS), F32), dots, dots,
            DMA((2, 4, 4)), DMA((2, 4, 4)), DMA((4,)), DMA((4, 4)), DMA((4, 4)), DMA((4, 4)),
            DMA((2, 4, 4)), DMA((2, 4, 4)), DMA((2, 4)), DMA((2, 4)), DMA((6,)),
            DMA((2,)), DMA((2,)), DMA((3, 8)), DMA((3,)), DMA((RING,)), DMA((RING,)),
        ],
        compiler_params=pltpu.CompilerParams(
            collective_id=0, has_side_effects=True, vmem_limit_bytes=64 * 1024 * 1024 - 65536
        ),
        name="step",
    )(frames_in, expert_ids.T, gate_values.T, gate_weight, up_weight, down_weight,
      norm_gain.reshape(1, D), pose_weight, target_pose, foot_contact.T)
    return (grad_input, gates_t.T, loss[0, 0])


def solution(mesh):
    in_specs = (
        P(("seg", "ep"), None),
        P(("seg", "ep"), None),
        P(("seg", "ep"), None),
        P("ep", None, None),
        P("ep", None, None),
        P("ep", None, None),
        P(),
        P(),
        P(("seg", "ep"), None),
        P(("seg", "ep"), None),
    )
    out_specs = (P(("seg", "ep"), None), P(("seg", "ep"), None), P())
    return jax.shard_map(
        per_device, mesh=mesh, in_specs=in_specs, out_specs=out_specs, check_vma=False
    )
```
